256 devices in a mesh: rows: 8 (over x, core), protos: 32 (over y, z).
Axes of the slice: x: 4, y: 4, z: 8, core: 2. Of those that a mesh axis runs over, the one named last changes fastest.
Arguments:
- teacher_features: bfloat16 [4096, 384], P(('rows', 'protos')), may hold values from -80 to 80, as said below
- student_features: bfloat16 [4096, 384], P(('rows', 'protos')), may hold values from -80 to 80, as said below
- prototypes: bfloat16 [131072, 384], P('protos'), may hold values from -80 to 80, as said below
Outputs:
- feature_grad: float32 [4096, 384], P(('rows', 'protos'))
- proto_grad: float32 [8, 16384, 384], P('rows', 'protos')
The draws below stay inside these ranges and needn't reach their ends.
Inputs may be any that keep to these rules, and one draw needn't show every extreme that they name: `teacher_features`: every row has nonzero entries. `student_features`: every row has nonzero entries. `prototypes`: every row has nonzero entries.
All inputs are finite; a program needn't handle non-finite values.
Results may differ from the reference program's by a relative error of at most 0.012.
The reference program's roundings to bfloat16 on the way (of `unit_t`, `unit_s`, `unit_w` and `delta`) count: a program that leaves them out, or rounds other values in their place, can miss the bound.
Values may be sent and summed in bfloat16 or wider, within the bound.
A program may use at most 64 MiB of HBM per device.

```python
import jax
import jax.numpy as jnp
from jax import lax

D = 384
K = 131072
PASSES = 3
ROWS = 4096
N_ROWS = 8
N_PROTOS = 32


cluster_count = 8


row_cuts = (96, 160, 200, 224, 238, 247, 252)


def centers(key):
    return jax.random.truncated_normal(jax.random.fold_in(key, 101), -4.0, 4.0, (cluster_count, D), jnp.float32)


def row_clusters(key):
    picks = jax.random.randint(jax.random.fold_in(key, 202), (ROWS,), 0, 256)
    cuts = jnp.array(row_cuts, jnp.int32)
    return jnp.sum((picks[:, None] >= cuts[None, :]).astype(jnp.int32), axis=1)


def mixed(key, groups, salt):
    count = groups.shape[0]
    noise_key = jax.random.fold_in(key, salt)
    base = jax.random.truncated_normal(noise_key, -4.0, 4.0, (count, D), jnp.float32)
    value = base + 0.6 * centers(key)[groups]
    return value


def draw_teacher_features(key, part):
    return mixed(key, row_clusters(key), 303).astype(jnp.bfloat16)


def draw_student_features(key, part):
    return mixed(key, row_clusters(key), 404).astype(jnp.bfloat16)


def draw_prototypes(key, part):
    spread = jax.random.randint(jax.random.fold_in(key, 505), (K,), 0, cluster_count)
    placed = jnp.arange(K, dtype=jnp.int32) * cluster_count // K
    choose = jax.random.randint(jax.random.fold_in(key, 507), (K,), 0, 4)
    groups = jnp.where(choose == 0, spread, placed).astype(jnp.int32)
    return mixed(key, groups, 606).astype(jnp.bfloat16)


def setup_inputs(seed: int = 0) -> dict:
    streams_of = jax.random.split(jax.random.key(seed), 4)
    teacher_features = draw_teacher_features(jax.random.fold_in(streams_of[3], 71), 0)
    student_features = draw_student_features(jax.random.fold_in(streams_of[3], 71), 0)
    prototypes = draw_prototypes(jax.random.fold_in(streams_of[3], 71), 0)
    return dict(teacher_features=teacher_features, student_features=student_features, prototypes=prototypes)


eps = 1e-06

def unitize(values):
    values = values.astype(jnp.float32)
    return (values * lax.rsqrt(lax.optimization_barrier(jnp.sum(values * values, axis=1, keepdims=True)) + eps)).astype(jnp.bfloat16)

def against(left, right):
    return lax.dot_general(left, right, (((1,), (1,)), ((), ())), preferred_element_type=jnp.float32)

def reference(teacher_features, student_features, prototypes):
    scale = 1.5 * D ** 0.5
    unit_t = unitize(teacher_features)
    unit_s = unitize(student_features)
    unit_w = unitize(prototypes)
    kernel = jnp.exp(scale * against(unit_t, unit_w))
    row_scale = jnp.ones((ROWS,), jnp.float32)
    col_scale = jnp.ones((K,), jnp.float32)
    for step in range(PASSES):
        col_scale = 1.0 / jnp.dot(row_scale, kernel, precision=lax.Precision.HIGHEST)
        row_scale = 1.0 / jnp.dot(kernel, col_scale, precision=lax.Precision.HIGHEST)
    factor = scale * K / ROWS
    block = min(ROWS, 256)
    pieces = []
    proto = jnp.zeros((K, D), jnp.float32)
    for begin in range(0, ROWS, block):
        target = kernel[begin:begin + block] * row_scale[begin:begin + block, None] * col_scale[None, :]
        powers = jnp.exp(scale * against(unit_s[begin:begin + block], unit_w))
        probs = powers / lax.optimization_barrier(jnp.sum(powers, axis=1, keepdims=True))
        delta = (probs - target).astype(jnp.bfloat16)
        pieces.append(scale * jnp.dot(delta, unit_w, preferred_element_type=jnp.float32))
        proto = proto + factor * lax.dot_general(delta, unit_s[begin:begin + block], (((0,), (0,)), ((), ())), preferred_element_type=jnp.float32)
    feature_grad = jnp.concatenate(pieces, axis=0)
    inner = K // (N_PROTOS * N_ROWS)
    proto_grad = proto.reshape(N_PROTOS, N_ROWS, inner, D).transpose(1, 0, 2, 3).reshape(N_ROWS, N_PROTOS * inner, D)
    return (feature_grad, proto_grad)
```

```python
import functools
import math

import jax
import jax.numpy as jnp
from jax import lax
from jax.experimental import pallas as pl
from jax.experimental.pallas import tpu as pltpu
from jax.sharding import PartitionSpec as P

K = 131072
PASSES = 3
EPS = 1e-06
LANES = 128
STEP = 256
CHIPS = 4
MESH = pl.DeviceIdType.MESH
f32 = jnp.float32
bf16 = jnp.bfloat16


def unitize(values):
    values = values.astype(f32)
    return (values * lax.rsqrt(jnp.sum(values * values, axis=1, keepdims=True) + EPS)).astype(bf16)


def kernel(
    n_rows, n_protos, factor_rows,
    t_ref, s_ref, w_ref, fg_ref, pg_ref,
    tg, sg, uw, km, pm, st, rb, qb, acc, cbuf, cvec, rbuf, qbuf,
    dbuf, feat, fsend, frecv, psend, precv, xsend, relay, xrecv, hold, own,
    t_ss, t_rs, s_ss, s_rs, c_ss, c_rs, r_ss, r_rs, q_ss, q_rs,
    p_ss, p_rs, x_ss, l_rs, x_rs, f_ss, f_rs,
):
    rows, protos = km.shape
    depth = uw.shape[1]
    block = t_ref.shape[0]
    chunk = protos // n_rows
    half = chunk // 2
    scale = 1.5 * math.sqrt(depth)
    power = scale * math.log2(math.e)
    factor = scale * K / factor_rows
    r = lax.axis_index("rows")
    p = lax.axis_index("protos")

    barrier = pltpu.get_barrier_semaphore()

    def greet(axis, me, count):
        def one(k, _):
            pl.semaphore_signal(
                barrier, inc=1, device_id={axis: lax.rem(me + k, count)}, device_id_type=MESH
            )
            return 0

        lax.fori_loop(1, count, one, 0)

    greet("protos", p, n_protos)
    greet("rows", r, n_rows)

    def spread(axis, me, count, source, target, send_sem, recv_sem):
        def one(k, _):
            pltpu.make_async_remote_copy(
                src_ref=source,
                dst_ref=target,
                send_sem=send_sem,
                recv_sem=recv_sem,
                device_id={axis: lax.rem(me + k, count)},
                device_id_type=MESH,
            ).start()
            return 0

        lax.fori_loop(1, count, one, 0)

    def drain(view, sem):
        pltpu.make_async_copy(view, view, sem).wait()

    tg[p] = unitize(t_ref[...])
    sg[p] = unitize(s_ref[...])
    pl.semaphore_wait(barrier, n_protos + n_rows - 2)
    spread("protos", p, n_protos, tg.at[p], tg.at[p], t_ss, t_rs)
    spread("protos", p, n_protos, sg.at[p], sg.at[p], s_ss, s_rs)

    def unit_step(i, _):
        at = pl.ds(pl.multiple_of(i * STEP, STEP), STEP)
        uw[at, :] = unitize(w_ref[at, :])
        return 0

    lax.fori_loop(0, protos // STEP, unit_step, 0)

    others = pl.ds(0, n_protos - 1)
    drain(tg.at[others], t_rs)

    def logits(left, i):
        at = pl.ds(pl.multiple_of(i * STEP, STEP), STEP)
        values = lax.dot_general(
            left, uw[at, :], (((1,), (1,)), ((), ())), preferred_element_type=f32
        )
        return at, jnp.exp2(values * power)

    teacher = tg[...].reshape(rows, depth)

    def kernel_step(i, _):
        at, values = logits(teacher, i)
        km[:, at] = values
        cbuf[0, r, :, at] = jnp.sum(values, axis=0, keepdims=True)
        return 0

    lax.fori_loop(0, protos // STEP, kernel_step, 0)

    def column(values):
        return jnp.transpose(jnp.broadcast_to(values, (LANES, LANES)))

    def to_columns(values, ref):
        for g in range(rows // LANES):
            ref[g * LANES:(g + 1) * LANES, :] = column(values[:, g * LANES:(g + 1) * LANES])

    def lane_sums(store):
        for g in range(rows // LANES):
            turned = jnp.transpose(acc[g * LANES:(g + 1) * LANES, :])
            store(slice(g * LANES, (g + 1) * LANES), jnp.sum(turned, axis=0, keepdims=True))

    tiles = protos // LANES

    def lane(j):
        return slice(j * LANES, (j + 1) * LANES)

    def column_pass(step):
        def one(i, sums):
            at = pl.ds(pl.multiple_of(i * 8, 8), 8)
            value = rb[at, :]
            return tuple(sums[j] + km[at, lane(j)] * value for j in range(tiles))

        sums = lax.fori_loop(
            0, rows // 8, one, tuple(jnp.zeros((8, LANES), f32) for _ in range(tiles)), unroll=2
        )
        for j in range(tiles):
            cbuf[step, r, :, lane(j)] = jnp.sum(sums[j], axis=0, keepdims=True)

    def row_pass(step):
        cols = [jnp.broadcast_to(cvec[:, lane(j)], (8, LANES)) for j in range(tiles)]

        def one(i, _):
            at = pl.ds(pl.multiple_of(i * 8, 8), 8)
            parts = [km[at, lane(j)] * cols[j] for j in range(4)]
            for j in range(4, tiles):
                parts[j % 4] = parts[j % 4] + km[at, lane(j)] * cols[j]
            acc[at, :] = (parts[0] + parts[1]) + (parts[2] + parts[3])
            return 0

        lax.fori_loop(0, rows // 8, one, 0, unroll=2)

        def store(at, value):
            rbuf[step, p, :, at] = value

        lane_sums(store)

    def student():
        drain(sg.at[others], s_rs)
        units = sg[...].reshape(rows, depth)
        acc[...] = jnp.zeros_like(acc)

        def one(i, _):
            at, values = logits(units, i)
            pm[:, at] = values
            acc[...] += values[:, :LANES] + values[:, LANES:]
            return 0

        lax.fori_loop(0, protos // STEP, one, 0)

        def store(at, value):
            qbuf[p, :, at] = value

        lane_sums(store)
        spread("protos", p, n_protos, qbuf.at[p], qbuf.at[p], q_ss, q_rs)
        st[...] = jnp.transpose(units.astype(f32)).astype(bf16)

    for step in range(PASSES):
        if step > 0:
            column_pass(step)
        spread(
            "rows", r, n_rows, cbuf.at[step, r], cbuf.at[step, r], c_ss.at[step], c_rs.at[step]
        )
        if step == 1:
            drain(qbuf.at[others], q_rs)
            to_columns(1.0 / jnp.sum(qbuf[...], axis=0), qb)
        drain(cbuf.at[step, pl.ds(0, n_rows - 1)], c_rs.at[step])
        cvec[...] = 1.0 / jnp.sum(cbuf[step], axis=0)
        row_pass(step)
        spread(
            "protos", p, n_protos, rbuf.at[step, p], rbuf.at[step, p], r_ss.at[step], r_rs.at[step]
        )
        if step == 0:
            student()
        drain(rbuf.at[step, others], r_rs.at[step])
        to_columns(1.0 / jnp.sum(rbuf[step], axis=0), rb)

    def term(owner, first):
        at = pl.ds(pl.multiple_of(owner * chunk, chunk), chunk)
        cols = cvec[:, at]

        def one(i, _):
            here = pl.ds(pl.multiple_of(i * 16, 16), 16)
            row = jnp.concatenate([rb[here, :]] * (chunk // LANES), axis=1)
            inv = jnp.concatenate([qb[here, :]] * (chunk // LANES), axis=1)
            delta = pm[here, at] * inv - km[here, at] * row * cols
            dbuf[here, :] = delta.astype(bf16)
            return 0

        lax.fori_loop(0, rows // 16, one, 0, unroll=2)
        delta = dbuf[...]
        part = jnp.dot(delta, uw[at, :], preferred_element_type=f32)
        if first:
            feat[...] = part
        else:
            feat[...] += part
        return jnp.dot(st[...], delta, preferred_element_type=f32)

    x, core = lax.div(r, 2), lax.rem(r, 2)

    def send(source, target, send_sem, recv_sem, to):
        pltpu.make_async_remote_copy(
            src_ref=source, dst_ref=target, send_sem=send_sem, recv_sem=recv_sem,
            device_id={"rows": to}, device_id_type=MESH,
        ).start()

    up = lax.rem(x + 1, CHIPS) * 2 + core
    down = lax.rem(x + CHIPS - 1, CHIPS) * 2 + core
    mate = x * 2 + 1 - core

    for k, ahead in enumerate((2, 1, 3, 0)):
        chip = lax.rem(x + ahead, CHIPS)
        part = term(chip * 2 + 1 - core, k == 0)
        psend[k, 0] = part[:, :half].astype(bf16)
        psend[k, 1] = part[:, half:].astype(bf16)
        send(psend.at[k], precv.at[k], p_ss.at[k], p_rs.at[k], mate)
        part = term(chip * 2 + core, False)
        drain(precv.at[k], p_rs.at[k])
        low = part[:, :half] + precv[k, 0].astype(f32)
        high = part[:, half:] + precv[k, 1].astype(f32)
        if k == 0:
            xsend[0, 0] = low.astype(bf16)
            xsend[0, 1] = high.astype(bf16)
            send(xsend.at[0, 0], relay.at[0], x_ss.at[0, 0], l_rs.at[0], up)
            send(xsend.at[0, 1], relay.at[1], x_ss.at[0, 1], l_rs.at[1], down)
        elif k == 1:
            hold[0] = low
            xsend[1, 1] = high.astype(bf16)
            send(xsend.at[1, 1], xrecv.at[0, 1], x_ss.at[1, 1], x_rs.at[0, 1], up)
        elif k == 2:
            hold[1] = high
            xsend[2, 0] = low.astype(bf16)
            send(xsend.at[2, 0], xrecv.at[1, 0], x_ss.at[2, 0], x_rs.at[1, 0], down)
        else:
            own[0] = low
            own[1] = high

    def feature_step(i, _):
        at = pl.ds(pl.multiple_of(i * block, block), block)
        fsend[i] = feat[at, :].astype(bf16)
        return 0

    lax.fori_loop(0, n_protos, feature_step, 0)

    def feature_send(k, _):
        q = lax.rem(p + k, n_protos)
        pltpu.make_async_remote_copy(
            src_ref=fsend.at[q], dst_ref=frecv.at[p], send_sem=f_ss, recv_sem=f_rs,
            device_id={"protos": q}, device_id_type=MESH,
        ).start()
        return 0

    lax.fori_loop(1, n_protos, feature_send, 0)
    frecv[p] = fsend[p]

    drain(relay.at[0], l_rs.at[0])
    xsend[1, 0] = (hold[0] + relay[0].astype(f32)).astype(bf16)
    send(xsend.at[1, 0], xrecv.at[0, 0], x_ss.at[1, 0], x_rs.at[0, 0], up)
    drain(relay.at[1], l_rs.at[1])
    xsend[2, 1] = (hold[1] + relay[1].astype(f32)).astype(bf16)
    send(xsend.at[2, 1], xrecv.at[1, 1], x_ss.at[2, 1], x_rs.at[1, 1], down)

    drain(frecv.at[others], f_rs)
    total = jnp.zeros((block, depth), f32)
    total = lax.fori_loop(0, n_protos, lambda i, a: a + frecv[i].astype(f32), total)
    fg_ref[...] = scale * total

    for side in range(2):
        for h in range(2):
            drain(xrecv.at[side, h], x_rs.at[side, h])
    for h in range(2):
        whole = own[h] + xrecv[0, h].astype(f32) + xrecv[1, h].astype(f32)
        pg_ref[h * half:(h + 1) * half, :] = jnp.transpose(factor * whole)

    drain(tg.at[others], t_ss)
    drain(sg.at[others], s_ss)
    drain(qbuf.at[others], q_ss)
    drain(frecv.at[others], f_ss)
    for step in range(PASSES):
        drain(cbuf.at[step, pl.ds(0, n_rows - 1)], c_ss.at[step])
        drain(rbuf.at[step, others], r_ss.at[step])
    for k in range(4):
        drain(psend.at[k], p_ss.at[k])
    for k in range(3):
        for h in range(2):
            drain(xsend.at[k, h], x_ss.at[k, h])


def on_device(teacher_features, student_features, prototypes):
    n_rows, n_protos = lax.axis_size("rows"), lax.axis_size("protos")
    block, depth = teacher_features.shape
    protos = prototypes.shape[0]
    rows = block * n_protos
    chunk = protos // n_rows
    half = chunk // 2
    dma = pltpu.SemaphoreType.DMA
    vmem = pltpu.VMEM
    feature_grad, proto_grad = pl.pallas_call(
        functools.partial(kernel, n_rows, n_protos, rows * n_rows),
        out_shape=(
            jax.ShapeDtypeStruct((block, depth), f32),
            jax.ShapeDtypeStruct((chunk, depth), f32),
        ),
        in_specs=[pl.BlockSpec(memory_space=pltpu.VMEM)] * 3,
        out_specs=(pl.BlockSpec(memory_space=pltpu.VMEM),) * 2,
        scratch_shapes=[
            vmem((n_protos, block, depth), bf16),
            vmem((n_protos, block, depth), bf16),
            vmem((protos, depth), bf16),
            vmem((rows, protos), f32),
            vmem((rows, protos), f32),
            vmem((depth, rows), bf16),
            vmem((rows, LANES), f32),
            vmem((rows, LANES), f32),
            vmem((rows, LANES), f32),
            vmem((PASSES, n_rows, 1, protos), f32),
            vmem((1, protos), f32),
            vmem((PASSES, n_protos, 1, rows), f32),
            vmem((n_protos, 1, rows), f32),
            vmem((rows, chunk), bf16),
            vmem((rows, depth), f32),
            vmem((n_protos, block, depth), bf16),
            vmem((n_protos, block, depth), bf16),
            vmem((4, 2, depth, half), bf16),
            vmem((4, 2, depth, half), bf16),
            vmem((3, 2, depth, half), bf16),
            vmem((2, depth, half), bf16),
            vmem((2, 2, depth, half), bf16),
            vmem((2, depth, half), f32),
            vmem((2, depth, half), f32),
            dma, dma, dma, dma,
            dma((PASSES,)), dma((PASSES,)), dma((PASSES,)), dma((PASSES,)),
            dma, dma,
            dma((4,)), dma((4,)),
            dma((3, 2)), dma((2,)), dma((2, 2)),
            dma, dma,
        ],
        compiler_params=pltpu.CompilerParams(
            collective_id=0, has_side_effects=True, vmem_limit_bytes=60 * 1024 * 1024
        ),
        name="head_step",
    )(teacher_features, student_features, prototypes)
    return feature_grad, proto_grad[None]


def solution(mesh):
    return jax.shard_map(
        on_device,
        mesh=mesh,
        in_specs=(P(("rows", "protos"), None), P(("rows", "protos"), None), P("protos", None)),
        out_specs=(P(("rows", "protos"), None), P("rows", "protos", None)),
        check_vma=False,
    )
```

```python
import functools
import math

import jax
import jax.numpy as jnp
from jax import lax
from jax.experimental import pallas as pl
from jax.experimental.pallas import tpu as pltpu
from jax.sharding import PartitionSpec as P

K = 131072
PASSES = 3
EPS = 1e-06
LANES = 128
STEP = 256
WIDE = 1024
MIDDLE = 512
CHIPS = 4
LINES = 4
MESH = pl.DeviceIdType.MESH
f32 = jnp.float32
bf16 = jnp.bfloat16


def unitize(values):
    values = values.astype(f32)
    return (values * lax.rsqrt(jnp.sum(values * values, axis=1, keepdims=True) + EPS)).astype(bf16)


def kernel(
    n_rows, n_protos, factor_rows,
    t_ref, s_ref, w_ref, fg_ref, pg_ref,
    tg, sg, uw, km, pm, st, rb, qb, acc, cbuf, cvec, rbuf, qbuf,
    wv, dall, fsend, fline, fout, frecv, psend, precv, xsend, relay, xrecv, hold, own,
    w_sem, t_ss, tz_rs, ty_rs, s_ss, sz_rs, sy_rs, c_ss, c_rs, r_ss, r_rs, q_ss, q_rs,
    p_ss, p_rs, x_ss, l_rs, x_rs, f_ss, fy_rs, g_ss, f_rs,
):
    rows, protos = km.shape
    depth = uw.shape[1]
    block = t_ref.shape[0]
    chunk = protos // n_rows
    half = chunk // 2
    scale = 1.5 * math.sqrt(depth)
    power = scale * math.log2(math.e)
    factor = scale * K / factor_rows
    r = lax.axis_index("rows")
    p = lax.axis_index("protos")

    barrier = pltpu.get_barrier_semaphore()

    depth_z = n_protos // LINES
    y, z = lax.div(p, depth_z), lax.rem(p, depth_z)
    x, core = lax.div(r, 2), lax.rem(r, 2)

    def spot(dy, dz):
        return lax.rem(y + dy, LINES) * depth_z + lax.rem(z + dz, depth_z)

    def far_first(j):
        return depth_z // 2 + lax.div(j + 1, 2) * (1 - 2 * lax.rem(j, 2))

    def remote(source, target, send_sem, recv_sem, to):
        pltpu.make_async_remote_copy(
            src_ref=source, dst_ref=target, send_sem=send_sem, recv_sem=recv_sem,
            device_id=to, device_id_type=MESH,
        ).start()

    def greet(to):
        pl.semaphore_signal(barrier, inc=1, device_id=to, device_id_type=MESH)

    def all_protos(visit):
        def one(j, _):
            for dy in (2, 1, 3, 0):
                visit(spot(dy, far_first(j)))
            return 0

        lax.fori_loop(0, depth_z - 1, one, 0)
        for dy in (2, 1, 3):
            visit(spot(dy, 0))

    def all_rows(visit):
        for ahead in (2, 1, 3):
            for other in range(2):
                visit(lax.rem(x + ahead, CHIPS) * 2 + lax.rem(core + other, 2))
        visit(x * 2 + 1 - core)

    all_protos(lambda q: greet({"protos": q}))
    all_rows(lambda q: greet({"rows": q}))

    def drain(view, sem):
        pltpu.make_async_copy(view, view, sem).wait()

    fetch = pltpu.make_async_copy(w_ref, wv, w_sem)
    fetch.start()
    tg[p] = unitize(t_ref[...])
    sg[p] = unitize(s_ref[...])
    pl.semaphore_wait(barrier, n_protos + n_rows - 2)

    def along_z(buf, send_sem, recv_sem):
        for j in range(depth_z - 1):
            dz = depth_z // 2 + (j + 1) // 2 * (1 - 2 * (j % 2))
            remote(
                buf.at[p], buf.at[p], send_sem, recv_sem.at[dz - 1], {"protos": spot(0, dz)}
            )

    def along_y(buf, q, send_sem, recv_sem, distances):
        for dy in distances:
            to = lax.rem(y + dy, LINES) * depth_z + z
            remote(buf.at[q], buf.at[q], send_sem, recv_sem.at[dy - 1], {"protos": to})

    def pass_on(buf, send_sem, z_sem, y_sem):
        along_y(buf, p, send_sem, y_sem, (1, 3))
        for j in reversed(range(depth_z - 1)):
            dz = depth_z // 2 + (j + 1) // 2 * (1 - 2 * (j % 2))
            q = spot(0, depth_z - dz)
            drain(buf.at[q], z_sem.at[dz - 1])
            along_y(buf, q, send_sem, y_sem, (1, 3))
        for k in range(depth_z):
            along_y(buf, y * depth_z + k, send_sem, y_sem, (2,))

    def column_here(buf, dy, y_sem):
        line = lax.rem(y + LINES - dy, LINES) * depth_z
        drain(buf.at[pl.ds(line, depth_z)], y_sem.at[dy - 1])

    along_z(tg, t_ss, tz_rs)
    along_z(sg, s_ss, sz_rs)
    fetch.wait()

    def unit_step(i, _):
        at = pl.ds(pl.multiple_of(i * STEP, STEP), STEP)
        uw[at, :] = unitize(wv[at, :])
        return 0

    lax.fori_loop(0, protos // STEP, unit_step, 0)

    others = pl.ds(0, n_protos - 1)
    pass_on(tg, t_ss, tz_rs, ty_rs)
    def logits(left, i, width):
        at = pl.ds(pl.multiple_of(i * width, width), width)
        values = lax.dot_general(
            left, uw[at, :], (((1,), (1,)), ((), ())), preferred_element_type=f32
        )
        return at, jnp.exp2(values * power)

    pair_rows = 2 * depth_z * block

    def kernel_half(pair, first):
        lines = pl.ds(pair * 2 * depth_z, 2 * depth_z)
        here = pl.ds(pl.multiple_of(pair * pair_rows, pair_rows), pair_rows)
        teacher = tg[lines].reshape(pair_rows, depth)

        def one(i, _):
            at, values = logits(teacher, i, WIDE)
            km[here, at] = values
            part = jnp.sum(values, axis=0, keepdims=True)
            cbuf[0, r, :, at] = part if first else cbuf[0, r, :, at] + part
            return 0

        lax.fori_loop(0, protos // WIDE, one, 0)

    odd = lax.rem(y, 2)
    near = 3 - 2 * odd
    line = lax.rem(y + LINES - near, LINES) * depth_z
    drain(tg.at[pl.ds(line, depth_z)], ty_rs.at[near - 1])
    kernel_half(lax.div(y, 2), True)
    pass_on(sg, s_ss, sz_rs, sy_rs)
    line = lax.rem(y + near, LINES) * depth_z
    drain(tg.at[pl.ds(line, depth_z)], ty_rs.at[LINES - near - 1])
    column_here(tg, 2, ty_rs)
    kernel_half(1 - lax.div(y, 2), False)

    def column(values):
        return jnp.transpose(jnp.broadcast_to(values, (LANES, LANES)))

    def to_columns(values, ref):
        for g in range(rows // LANES):
            ref[g * LANES:(g + 1) * LANES, :] = column(values[:, g * LANES:(g + 1) * LANES])

    def lane_sums(acc, store):
        for g in range(rows // LANES):
            turned = jnp.transpose(acc[g * LANES:(g + 1) * LANES, :])
            store(slice(g * LANES, (g + 1) * LANES), jnp.sum(turned, axis=0, keepdims=True))

    tiles = protos // LANES

    def lane(j):
        return slice(j * LANES, (j + 1) * LANES)

    def column_pass(step):
        def one(i, sums):
            at = pl.ds(pl.multiple_of(i * 8, 8), 8)
            value = rb[at, :]
            return tuple(sums[j] + km[at, lane(j)] * value for j in range(tiles))

        sums = lax.fori_loop(
            0, rows // 8, one, tuple(jnp.zeros((8, LANES), f32) for _ in range(tiles)), unroll=2
        )
        for j in range(tiles):
            cbuf[step, r, :, lane(j)] = jnp.sum(sums[j], axis=0, keepdims=True)

    def row_pass(step):
        cols = [jnp.broadcast_to(cvec[:, lane(j)], (8, LANES)) for j in range(tiles)]

        def one(i, _):
            at = pl.ds(pl.multiple_of(i * 8, 8), 8)
            parts = [km[at, lane(j)] * cols[j] for j in range(4)]
            for j in range(4, tiles):
                parts[j % 4] = parts[j % 4] + km[at, lane(j)] * cols[j]
            acc[at, :] = (parts[0] + parts[1]) + (parts[2] + parts[3])
            return 0

        lax.fori_loop(0, rows // 8, one, 0, unroll=2)

        def store(at, value):
            rbuf[step, p, :, at] = value

        lane_sums(acc, store)

    steps = protos // MIDDLE

    def student(begin, end):
        units = sg[...].reshape(rows, depth)

        def one(i, _):
            at, values = logits(units, i, MIDDLE)
            pm[:, at] = values
            qb[...] += sum(values[:, j * LANES:(j + 1) * LANES] for j in range(MIDDLE // LANES))
            return 0

        lax.fori_loop(begin, end, one, 0)

    def student_begin():
        for dy in (1, 2, 3):
            column_here(sg, dy, sy_rs)
        qb[...] = jnp.zeros_like(qb)
        student(0, steps // 2)

    def student_end():
        student(steps // 2, steps)

        def store(at, value):
            qbuf[p, :, at] = value

        lane_sums(qb, store)
        all_protos(lambda q: remote(qbuf.at[p], qbuf.at[p], q_ss, q_rs, {"protos": q}))

    for step in range(PASSES):
        if step > 0:
            column_pass(step)
        mine = cbuf.at[step, r]
        all_rows(lambda q: remote(mine, mine, c_ss.at[step], c_rs.at[step], {"rows": q}))
        if step == 1:
            student_end()
        elif step == 2:
            drain(qbuf.at[others], q_rs)
            to_columns(1.0 / jnp.sum(qbuf[...], axis=0), qb)
        drain(cbuf.at[step, pl.ds(0, n_rows - 1)], c_rs.at[step])
        cvec[...] = 1.0 / jnp.sum(cbuf[step], axis=0)
        row_pass(step)
        mine = rbuf.at[step, p]
        all_protos(lambda q: remote(mine, mine, r_ss.at[step], r_rs.at[step], {"protos": q}))
        if step == 0:
            student_begin()
        elif step == 1:
            st[...] = jnp.transpose(sg[...].reshape(rows, depth).astype(f32)).astype(bf16)
        drain(rbuf.at[step, others], r_rs.at[step])
        to_columns(1.0 / jnp.sum(rbuf[step], axis=0), rb)

    def delta(owner):
        at = pl.ds(pl.multiple_of(owner * chunk, chunk), chunk)
        cols = cvec[:, at]

        def one(i, _):
            here = pl.ds(pl.multiple_of(i * 16, 16), 16)
            row = jnp.concatenate([rb[here, :]] * (chunk // LANES), axis=1)
            inv = jnp.concatenate([qb[here, :]] * (chunk // LANES), axis=1)
            value = pm[here, at] * inv - km[here, at] * row * cols
            dall[here, at] = value.astype(bf16)
            return 0

        lax.fori_loop(0, rows // 16, one, 0, unroll=2)

    def term(owner):
        at = pl.ds(pl.multiple_of(owner * chunk, chunk), chunk)
        return jnp.dot(st[...], dall[:, at], preferred_element_type=f32)

    def features():
        half_rows = rows // 2

        def one(i, _):
            here = pl.ds(pl.multiple_of(i * half_rows, half_rows), half_rows)
            part = jnp.dot(dall[here, :], uw[...], preferred_element_type=f32).astype(bf16)
            to = pl.ds(i * (n_protos // 2), n_protos // 2)
            fsend[to] = part.reshape(n_protos // 2, block, depth)
            return 0

        lax.fori_loop(0, 2, one, 0)

        def post(j, _):
            dz = far_first(j)
            for dy in (2, 1, 3):
                q = spot(dy, dz)
                to = lax.rem(y + dy, LINES) * depth_z + z
                remote(fsend.at[q], fline.at[j, dy - 1], f_ss, fy_rs.at[j], {"protos": to})
            return 0

        lax.fori_loop(0, depth_z, post, 0)

    def features_on():
        def one(j, _):
            q = spot(0, far_first(j))
            drain(fline.at[j], fy_rs.at[j])
            value = fsend[q].astype(f32) + fline[j, 0].astype(f32)
            value = value + (fline[j, 1].astype(f32) + fline[j, 2].astype(f32))
            fout[j] = value.astype(bf16)
            return 0

        def step(j, _):
            one(j, 0)
            q = spot(0, far_first(j))
            remote(fout.at[j], frecv.at[z], g_ss, f_rs, {"protos": q})
            return 0

        lax.fori_loop(0, depth_z - 1, step, 0)
        one(depth_z - 1, 0)
        frecv[z] = fout[depth_z - 1]

    def send(source, target, send_sem, recv_sem, to):
        remote(source, target, send_sem, recv_sem, {"rows": to})

    up = lax.rem(x + 1, CHIPS) * 2 + core
    down = lax.rem(x + CHIPS - 1, CHIPS) * 2 + core
    mate = x * 2 + 1 - core

    chips = [lax.rem(x + ahead, CHIPS) for ahead in (2, 1, 3, 0)]

    def to_mate(k):
        part = term(chips[k] * 2 + 1 - core)
        psend[k, 0] = part[:, :half].astype(bf16)
        psend[k, 1] = part[:, half:].astype(bf16)
        send(psend.at[k], precv.at[k], p_ss.at[k], p_rs.at[k], mate)

    def with_mate(k):
        part = term(chips[k] * 2 + core)
        drain(precv.at[k], p_rs.at[k])
        return part[:, :half] + precv[k, 0].astype(f32), part[:, half:] + precv[k, 1].astype(f32)

    delta(chips[0] * 2 + 1 - core)
    to_mate(0)
    delta(chips[0] * 2 + core)
    low, high = with_mate(0)
    xsend[0, 0] = low.astype(bf16)
    xsend[0, 1] = high.astype(bf16)
    send(xsend.at[0, 0], relay.at[0], x_ss.at[0, 0], l_rs.at[0], up)
    send(xsend.at[0, 1], relay.at[1], x_ss.at[0, 1], l_rs.at[1], down)
    def deltas(k):
        delta(chips[k] * 2 + 1 - core)
        delta(chips[k] * 2 + core)

    deltas(1)
    to_mate(1)
    deltas(2)
    to_mate(2)
    low, high = with_mate(1)
    hold[0] = low
    xsend[1, 1] = high.astype(bf16)
    send(xsend.at[1, 1], xrecv.at[0, 1], x_ss.at[1, 1], x_rs.at[0, 1], up)
    low, high = with_mate(2)
    hold[1] = high
    xsend[2, 0] = low.astype(bf16)
    send(xsend.at[2, 0], xrecv.at[1, 0], x_ss.at[2, 0], x_rs.at[1, 0], down)
    deltas(3)
    features()
    to_mate(3)
    low, high = with_mate(3)
    own[0] = low
    own[1] = high

    drain(relay.at[0], l_rs.at[0])
    xsend[1, 0] = (hold[0] + relay[0].astype(f32)).astype(bf16)
    send(xsend.at[1, 0], xrecv.at[0, 0], x_ss.at[1, 0], x_rs.at[0, 0], up)
    drain(relay.at[1], l_rs.at[1])
    xsend[2, 1] = (hold[1] + relay[1].astype(f32)).astype(bf16)
    send(xsend.at[2, 1], xrecv.at[1, 1], x_ss.at[2, 1], x_rs.at[1, 1], down)

    features_on()
    drain(frecv.at[pl.ds(0, depth_z - 1)], f_rs)
    total = jnp.zeros((block, depth), f32)
    total = lax.fori_loop(0, depth_z, lambda i, a: a + frecv[i].astype(f32), total)
    fg_ref[...] = scale * total

    for side in range(2):
        for h in range(2):
            drain(xrecv.at[side, h], x_rs.at[side, h])
    for h in range(2):
        whole = own[h] + xrecv[0, h].astype(f32) + xrecv[1, h].astype(f32)
        pg_ref[h * half:(h + 1) * half, :] = jnp.transpose(factor * whole)

    drain(tg.at[others], t_ss)
    drain(sg.at[others], s_ss)
    drain(qbuf.at[others], q_ss)
    drain(fline, f_ss)
    drain(frecv.at[pl.ds(0, depth_z - 1)], g_ss)
    for step in range(PASSES):
        drain(cbuf.at[step, pl.ds(0, n_rows - 1)], c_ss.at[step])
        drain(rbuf.at[step, others], r_ss.at[step])
    for k in range(4):
        drain(psend.at[k], p_ss.at[k])
    for k in range(3):
        for h in range(2):
            drain(xsend.at[k, h], x_ss.at[k, h])


def on_device(teacher_features, student_features, prototypes):
    n_rows, n_protos = lax.axis_size("rows"), lax.axis_size("protos")
    block, depth = teacher_features.shape
    protos = prototypes.shape[0]
    rows = block * n_protos
    chunk = protos // n_rows
    half = chunk // 2
    depth_z = n_protos // LINES
    dma = pltpu.SemaphoreType.DMA
    vmem = pltpu.VMEM
    feature_grad, proto_grad = pl.pallas_call(
        functools.partial(kernel, n_rows, n_protos, rows * n_rows),
        out_shape=(
            jax.ShapeDtypeStruct((block, depth), f32),
            jax.ShapeDtypeStruct((chunk, depth), f32),
        ),
        in_specs=[pl.BlockSpec(memory_space=pltpu.VMEM)] * 2 + [pl.BlockSpec(memory_space=pl.ANY)],
        out_specs=(pl.BlockSpec(memory_space=pltpu.VMEM),) * 2,
        scratch_shapes=[
            vmem((n_protos, block, depth), bf16),
            vmem((n_protos, block, depth), bf16),
            vmem((protos, depth), bf16),
            vmem((rows, protos), f32),
            vmem((rows, protos), f32),
            vmem((depth, rows), bf16),
            vmem((rows, LANES), f32),
            vmem((rows, LANES), f32),
            vmem((rows, LANES), f32),
            vmem((PASSES, n_rows, 1, protos), f32),
            vmem((1, protos), f32),
            vmem((PASSES, n_protos, 1, rows), f32),
            vmem((n_protos, 1, rows), f32),
            vmem((protos, depth), bf16),
            vmem((rows, protos), bf16),
            vmem((n_protos, block, depth), bf16),
            vmem((depth_z, LINES - 1, block, depth), bf16),
            vmem((depth_z, block, depth), bf16),
            vmem((depth_z, block, depth), bf16),
            vmem((4, 2, depth, half), bf16),
            vmem((4, 2, depth, half), bf16),
            vmem((3, 2, depth, half), bf16),
            vmem((2, depth, half), bf16),
            vmem((2, 2, depth, half), bf16),
            vmem((2, depth, half), f32),
            vmem((2, depth, half), f32),
            dma, dma, dma((depth_z - 1,)), dma((LINES - 1,)),
            dma, dma((depth_z - 1,)), dma((LINES - 1,)),
            dma((PASSES,)), dma((PASSES,)), dma((PASSES,)), dma((PASSES,)),
            dma, dma,
            dma((4,)), dma((4,)),
            dma((3, 2)), dma((2,)), dma((2, 2)),
            dma, dma((depth_z,)), dma, dma,
        ],
        compiler_params=pltpu.CompilerParams(
            collective_id=0, has_side_effects=True, vmem_limit_bytes=60 * 1024 * 1024
        ),
        name="head_step",
    )(teacher_features, student_features, prototypes)
    return feature_grad, proto_grad[None]


def solution(mesh):
    return jax.shard_map(
        on_device,
        mesh=mesh,
        in_specs=(P(("rows", "protos"), None), P(("rows", "protos"), None), P("protos", None)),
        out_specs=(P(("rows", "protos"), None), P("rows", "protos", None)),
        check_vma=False,
    )
```

```python
import functools
import math

import jax
import jax.numpy as jnp
from jax import lax
from jax.experimental import pallas as pl
from jax.experimental.pallas import tpu as pltpu
from jax.sharding import PartitionSpec as P

K = 131072
PASSES = 3
EPS = 1e-06
LANES = 128
STEP = 256
WIDE = 1024
MIDDLE = 512
CHIPS = 4
LINES = 4
MESH = pl.DeviceIdType.MESH
f32 = jnp.float32
bf16 = jnp.bfloat16


def unitize(values):
    values = values.astype(f32)
    return (values * lax.rsqrt(jnp.sum(values * values, axis=1, keepdims=True) + EPS)).astype(bf16)


def kernel(
    n_rows, n_protos, factor_rows,
    t_hbm, s_hbm, w_ref, fg_ref, pg_ref,
    tg, sg, uw, km, pm, st, rb, qb, acc, cacc, cbuf, cvec, rbuf, qbuf,
    wv, t_ref, s_ref, dall, fsend, fline, fout, frecv, psend, precv, xsend, relay, xrecv, hold, own,
    in_sem, t_ss, tz_rs, ty_rs, s_ss, sz_rs, sy_rs, c_ss, c_rs, r_ss, r_rs, q_ss, q_rs,
    p_ss, p_rs, x_ss, l_rs, x_rs, f_ss, fy_rs, g_ss, f_rs,
):
    rows, protos = km.shape
    depth = uw.shape[1]
    block = t_ref.shape[0]
    chunk = protos // n_rows
    half = chunk // 2
    scale = 1.5 * math.sqrt(depth)
    power = scale * math.log2(math.e)
    factor = scale * K / factor_rows
    r = lax.axis_index("rows")
    p = lax.axis_index("protos")

    loads = [
        pltpu.make_async_copy(source, target, in_sem.at[k])
        for k, (source, target) in enumerate(((t_hbm, t_ref), (s_hbm, s_ref), (w_ref, wv)))
    ]
    for copy in loads:
        copy.start()

    barrier = pltpu.get_barrier_semaphore()

    depth_z = n_protos // LINES
    y, z = lax.div(p, depth_z), lax.rem(p, depth_z)
    x, core = lax.div(r, 2), lax.rem(r, 2)

    def spot(dy, dz):
        return lax.rem(y + dy, LINES) * depth_z + lax.rem(z + dz, depth_z)

    def far_first(j):
        return depth_z // 2 + lax.div(j + 1, 2) * (1 - 2 * lax.rem(j, 2))

    def remote(source, target, send_sem, recv_sem, to):
        pltpu.make_async_remote_copy(
            src_ref=source, dst_ref=target, send_sem=send_sem, recv_sem=recv_sem,
            device_id=to, device_id_type=MESH,
        ).start()

    def greet(to):
        pl.semaphore_signal(barrier, inc=1, device_id=to, device_id_type=MESH)

    def all_protos(visit):
        def one(j, _):
            for dy in (2, 1, 3, 0):
                visit(spot(dy, far_first(j)))
            return 0

        lax.fori_loop(0, depth_z - 1, one, 0)
        for dy in (2, 1, 3):
            visit(spot(dy, 0))

    def all_rows(visit):
        for ahead in (2, 1, 3):
            for other in range(2):
                visit(lax.rem(x + ahead, CHIPS) * 2 + lax.rem(core + other, 2))
        visit(x * 2 + 1 - core)

    all_protos(lambda q: greet({"protos": q}))
    all_rows(lambda q: greet({"rows": q}))

    def drain(view, sem):
        pltpu.make_async_copy(view, view, sem).wait()

    for copy in loads[:2]:
        copy.wait()
    tg[p] = unitize(t_ref[...])
    sg[p] = unitize(s_ref[...])
    pl.semaphore_wait(barrier, n_protos + n_rows - 2)

    def along_z(buf, send_sem, recv_sem):
        for j in range(depth_z - 1):
            dz = depth_z // 2 + (j + 1) // 2 * (1 - 2 * (j % 2))
            remote(
                buf.at[p], buf.at[p], send_sem, recv_sem.at[dz - 1], {"protos": spot(0, dz)}
            )

    def along_y(buf, q, send_sem, recv_sem, distances):
        for dy in distances:
            to = lax.rem(y + dy, LINES) * depth_z + z
            remote(buf.at[q], buf.at[q], send_sem, recv_sem.at[dy - 1], {"protos": to})

    def pass_on(buf, send_sem, z_sem, y_sem):
        along_y(buf, p, send_sem, y_sem, (1, 3))
        for j in reversed(range(depth_z - 1)):
            dz = depth_z // 2 + (j + 1) // 2 * (1 - 2 * (j % 2))
            q = spot(0, depth_z - dz)
            drain(buf.at[q], z_sem.at[dz - 1])
            along_y(buf, q, send_sem, y_sem, (1, 3))
        for k in range(depth_z):
            along_y(buf, y * depth_z + k, send_sem, y_sem, (2,))

    def column_here(buf, dy, y_sem):
        line = lax.rem(y + LINES - dy, LINES) * depth_z
        drain(buf.at[pl.ds(line, depth_z)], y_sem.at[dy - 1])

    along_z(tg, t_ss, tz_rs)
    along_z(sg, s_ss, sz_rs)
    loads[2].wait()

    def unit_step(i, _):
        at = pl.ds(pl.multiple_of(i * STEP, STEP), STEP)
        uw[at, :] = unitize(wv[at, :])
        return 0

    lax.fori_loop(0, protos // STEP, unit_step, 0)

    others = pl.ds(0, n_protos - 1)
    pass_on(tg, t_ss, tz_rs, ty_rs)
    def logits(left, i, width):
        at = pl.ds(pl.multiple_of(i * width, width), width)
        values = lax.dot_general(
            left, uw[at, :], (((1,), (1,)), ((), ())), preferred_element_type=f32
        )
        return at, jnp.exp2(values * power)

    pair_rows = 2 * depth_z * block

    def kernel_half(pair, c, first):
        lines = pl.ds(pair * 2 * depth_z, 2 * depth_z)
        here = pl.ds(pl.multiple_of(pair * pair_rows, pair_rows), pair_rows)
        teacher = tg[lines].reshape(pair_rows, depth)
        steps = protos // 2 // WIDE

        def one(i, _):
            at, values = logits(teacher, c * steps + i, WIDE)
            km[here, at] = values
            part = jnp.sum(values, axis=0, keepdims=True)
            to = pl.ds(pl.multiple_of(i * WIDE, WIDE), WIDE)
            cbuf[0, c, r, :, to] = part if first else cbuf[0, c, r, :, to] + part
            return 0

        lax.fori_loop(0, steps, one, 0)

    odd = lax.rem(y, 2)
    near = 3 - 2 * odd
    line = lax.rem(y + LINES - near, LINES) * depth_z
    drain(tg.at[pl.ds(line, depth_z)], ty_rs.at[near - 1])
    kernel_half(lax.div(y, 2), 0, True)
    kernel_half(lax.div(y, 2), 1, True)
    pass_on(sg, s_ss, sz_rs, sy_rs)
    line = lax.rem(y + near, LINES) * depth_z
    drain(tg.at[pl.ds(line, depth_z)], ty_rs.at[LINES - near - 1])
    column_here(tg, 2, ty_rs)

    def column(values):
        return jnp.transpose(jnp.broadcast_to(values, (LANES, LANES)))

    def to_columns(values, ref):
        for g in range(rows // LANES):
            ref[g * LANES:(g + 1) * LANES, :] = column(values[:, g * LANES:(g + 1) * LANES])

    def lane_sums(acc, store, groups):
        for g in groups:
            turned = jnp.transpose(acc[g * LANES:(g + 1) * LANES, :])
            at = slice((g - groups[0]) * LANES, (g - groups[0] + 1) * LANES)
            store(at, jnp.sum(turned, axis=0, keepdims=True))

    tiles = protos // LANES
    groups = rows // LANES
    side = protos // 2
    wing = rows // 2

    def lane(j):
        return slice(j * LANES, (j + 1) * LANES)

    def rows_of(i):
        return pl.ds(pl.multiple_of(i * 8, 8), 8)

    def column_sweep(h, which):
        def one(i, sums):
            at = rows_of(i)
            value = rb[at, :]
            return tuple(s + km[at, lane(j)] * value for s, j in zip(sums, which))

        return lax.fori_loop(
            h * wing // 8, (h + 1) * wing // 8, one,
            tuple(jnp.zeros((8, LANES), f32) for _ in which), unroll=2,
        )

    def row_sweep(h, c):
        which = range(c * tiles // 2, (c + 1) * tiles // 2)
        cols = [jnp.broadcast_to(cvec[:, lane(j)], (8, LANES)) for j in which]

        def one(i, _):
            at = rows_of(i)
            parts = [km[at, lane(j)] * col for j, col in zip(which[:4], cols[:4])]
            for k in range(4, len(which)):
                parts[k % 4] = parts[k % 4] + km[at, lane(which[k])] * cols[k]
            total = (parts[0] + parts[1]) + (parts[2] + parts[3])
            acc[at, :] = total if c == 0 else acc[at, :] + total
            return 0

        lax.fori_loop(h * wing // 8, (h + 1) * wing // 8, one, 0, unroll=2)

    def send_columns(step, c):
        mine = cbuf.at[step, c, r]
        sems = c_ss.at[step, c], c_rs.at[step, c]
        all_rows(lambda q: remote(mine, mine, *sems, {"rows": q}))

    def send_sums(step, h):
        mine = rbuf.at[step, h, p]
        sems = r_ss.at[step, h], r_rs.at[step, h]
        all_protos(lambda q: remote(mine, mine, *sems, {"protos": q}))

    def take_columns(step, c):
        drain(cbuf.at[step, c, pl.ds(0, n_rows - 1)], c_rs.at[step, c])
        cvec[:, c * side:(c + 1) * side] = 1.0 / jnp.sum(cbuf[step, c], axis=0)

    def take_sums(step, h):
        drain(rbuf.at[step, h, others], r_rs.at[step, h])
        values = 1.0 / jnp.sum(rbuf[step, h], axis=0)
        for g in range(groups // 2):
            at = h * wing + g * LANES
            rb[at:at + LANES, :] = column(values[:, lane(g)])

    def column_pass(step):
        take_sums(step - 1, 0)
        for j, value in enumerate(column_sweep(0, range(tiles))):
            cacc[:, lane(j)] = value
        take_sums(step - 1, 1)
        for c in range(2):
            which = range(c * tiles // 2, (c + 1) * tiles // 2)
            for j, value in zip(which, column_sweep(1, which)):
                value = jnp.sum(value + cacc[:, lane(j)], axis=0, keepdims=True)
                cbuf[step, c, r, :, lane(j - which[0])] = value
            send_columns(step, c)

    def row_pass(step):
        take_columns(step, 0)
        row_sweep(0, 0)
        row_sweep(1, 0)
        take_columns(step, 1)
        for h in range(2):
            row_sweep(h, 1)

            def store(at, value):
                rbuf[step, h, p, :, at] = value

            lane_sums(acc, store, range(h * groups // 2, (h + 1) * groups // 2))
            send_sums(step, h)

    steps = protos // MIDDLE

    def student(begin, end):
        units = sg[...].reshape(rows, depth)

        def one(i, _):
            at, values = logits(units, i, MIDDLE)
            pm[:, at] = values
            qb[...] += sum(values[:, j * LANES:(j + 1) * LANES] for j in range(MIDDLE // LANES))
            return 0

        lax.fori_loop(begin, end, one, 0)

    def student_begin():
        for dy in (1, 2, 3):
            column_here(sg, dy, sy_rs)
        qb[...] = jnp.zeros_like(qb)
        student(0, steps // 2)

    def student_end():
        student(steps // 2, steps)

        def store(at, value):
            qbuf[p, :, at] = value

        lane_sums(qb, store, range(groups))
        all_protos(lambda q: remote(qbuf.at[p], qbuf.at[p], q_ss, q_rs, {"protos": q}))

    for c in range(2):
        kernel_half(1 - lax.div(y, 2), c, False)
        send_columns(0, c)

    for step in range(PASSES):
        if step > 0:
            column_pass(step)
        if step == 1:
            student_end()
        elif step == 2:
            drain(qbuf.at[others], q_rs)
            to_columns(1.0 / jnp.sum(qbuf[...], axis=0), qb)
        row_pass(step)
        if step == 0:
            student_begin()
        elif step == 1:
            st[...] = jnp.transpose(sg[...].reshape(rows, depth).astype(f32)).astype(bf16)
    for h in range(2):
        take_sums(PASSES - 1, h)

    def delta(owner):
        at = pl.ds(pl.multiple_of(owner * chunk, chunk), chunk)
        cols = cvec[:, at]

        def one(i, _):
            here = pl.ds(pl.multiple_of(i * 16, 16), 16)
            row = jnp.concatenate([rb[here, :]] * (chunk // LANES), axis=1)
            inv = jnp.concatenate([qb[here, :]] * (chunk // LANES), axis=1)
            value = pm[here, at] * inv - km[here, at] * row * cols
            dall[here, at] = value.astype(bf16)
            return 0

        lax.fori_loop(0, rows // 16, one, 0, unroll=2)

    def term(owner):
        at = pl.ds(pl.multiple_of(owner * chunk, chunk), chunk)
        return jnp.dot(st[...], dall[:, at], preferred_element_type=f32)

    def features():
        half_rows = rows // 2

        def one(i, _):
            here = pl.ds(pl.multiple_of(i * half_rows, half_rows), half_rows)
            part = jnp.dot(dall[here, :], uw[...], preferred_element_type=f32).astype(bf16)
            to = pl.ds(i * (n_protos // 2), n_protos // 2)
            fsend[to] = part.reshape(n_protos // 2, block, depth)
            return 0

        lax.fori_loop(0, 2, one, 0)

        def post(j, _):
            dz = far_first(j)
            for dy in (2, 1, 3):
                q = spot(dy, dz)
                to = lax.rem(y + dy, LINES) * depth_z + z
                remote(fsend.at[q], fline.at[j, dy - 1], f_ss, fy_rs.at[j], {"protos": to})
            return 0

        lax.fori_loop(0, depth_z, post, 0)

    def features_on():
        def one(j, _):
            q = spot(0, far_first(j))
            drain(fline.at[j], fy_rs.at[j])
            value = fsend[q].astype(f32) + fline[j, 0].astype(f32)
            value = value + (fline[j, 1].astype(f32) + fline[j, 2].astype(f32))
            fout[j] = value.astype(bf16)
            return 0

        def step(j, _):
            one(j, 0)
            q = spot(0, far_first(j))
            remote(fout.at[j], frecv.at[z], g_ss, f_rs, {"protos": q})
            return 0

        lax.fori_loop(0, depth_z - 1, step, 0)
        one(depth_z - 1, 0)
        frecv[z] = fout[depth_z - 1]

    def send(source, target, send_sem, recv_sem, to):
        remote(source, target, send_sem, recv_sem, {"rows": to})

    up = lax.rem(x + 1, CHIPS) * 2 + core
    down = lax.rem(x + CHIPS - 1, CHIPS) * 2 + core
    mate = x * 2 + 1 - core

    chips = [lax.rem(x + ahead, CHIPS) for ahead in (2, 1, 3, 0)]

    def to_mate(k):
        part = term(chips[k] * 2 + 1 - core)
        psend[k, 0] = part[:, :half].astype(bf16)
        psend[k, 1] = part[:, half:].astype(bf16)
        send(psend.at[k], precv.at[k], p_ss.at[k], p_rs.at[k], mate)

    def with_mate(k):
        part = term(chips[k] * 2 + core)
        drain(precv.at[k], p_rs.at[k])
        return part[:, :half] + precv[k, 0].astype(f32), part[:, half:] + precv[k, 1].astype(f32)

    delta(chips[0] * 2 + 1 - core)
    to_mate(0)
    delta(chips[0] * 2 + core)
    low, high = with_mate(0)
    xsend[0, 0] = low.astype(bf16)
    xsend[0, 1] = high.astype(bf16)
    send(xsend.at[0, 0], relay.at[0], x_ss.at[0, 0], l_rs.at[0], up)
    send(xsend.at[0, 1], relay.at[1], x_ss.at[0, 1], l_rs.at[1], down)
    def deltas(k):
        delta(chips[k] * 2 + 1 - core)
        delta(chips[k] * 2 + core)

    deltas(1)
    to_mate(1)
    deltas(2)
    to_mate(2)
    low, high = with_mate(1)
    hold[0] = low
    xsend[1, 1] = high.astype(bf16)
    send(xsend.at[1, 1], xrecv.at[0, 1], x_ss.at[1, 1], x_rs.at[0, 1], up)
    low, high = with_mate(2)
    hold[1] = high
    xsend[2, 0] = low.astype(bf16)
    send(xsend.at[2, 0], xrecv.at[1, 0], x_ss.at[2, 0], x_rs.at[1, 0], down)
    deltas(3)
    features()
    to_mate(3)
    low, high = with_mate(3)
    own[0] = low
    own[1] = high

    drain(relay.at[0], l_rs.at[0])
    xsend[1, 0] = (hold[0] + relay[0].astype(f32)).astype(bf16)
    send(xsend.at[1, 0], xrecv.at[0, 0], x_ss.at[1, 0], x_rs.at[0, 0], up)
    drain(relay.at[1], l_rs.at[1])
    xsend[2, 1] = (hold[1] + relay[1].astype(f32)).astype(bf16)
    send(xsend.at[2, 1], xrecv.at[1, 1], x_ss.at[2, 1], x_rs.at[1, 1], down)

    features_on()
    drain(frecv.at[pl.ds(0, depth_z - 1)], f_rs)
    total = jnp.zeros((block, depth), f32)
    total = lax.fori_loop(0, depth_z, lambda i, a: a + frecv[i].astype(f32), total)
    fg_ref[...] = scale * total

    for side in range(2):
        for h in range(2):
            drain(xrecv.at[side, h], x_rs.at[side, h])
    for h in range(2):
        whole = own[h] + xrecv[0, h].astype(f32) + xrecv[1, h].astype(f32)
        pg_ref[h * half:(h + 1) * half, :] = jnp.transpose(factor * whole)

    drain(tg.at[others], t_ss)
    drain(sg.at[others], s_ss)
    drain(qbuf.at[others], q_ss)
    drain(fline, f_ss)
    drain(frecv.at[pl.ds(0, depth_z - 1)], g_ss)
    for step in range(PASSES):
        for h in range(2):
            drain(cbuf.at[step, h, pl.ds(0, n_rows - 1)], c_ss.at[step, h])
            drain(rbuf.at[step, h, others], r_ss.at[step, h])
    for k in range(4):
        drain(psend.at[k], p_ss.at[k])
    for k in range(3):
        for h in range(2):
            drain(xsend.at[k, h], x_ss.at[k, h])


def store(feature, proto, feature_out, proto_out, f_sem, p_sem):
    copies = [
        pltpu.make_async_copy(proto, proto_out, p_sem),
        pltpu.make_async_copy(feature, feature_out, f_sem),
    ]
    for copy in copies:
        copy.start()
    for copy in copies:
        copy.wait()


def on_device(teacher_features, student_features, prototypes):
    n_rows, n_protos = lax.axis_size("rows"), lax.axis_size("protos")
    block, depth = teacher_features.shape
    protos = prototypes.shape[0]
    rows = block * n_protos
    chunk = protos // n_rows
    half = chunk // 2
    depth_z = n_protos // LINES
    dma = pltpu.SemaphoreType.DMA
    vmem = pltpu.VMEM
    feature_grad, proto_grad = pl.pallas_call(
        functools.partial(kernel, n_rows, n_protos, rows * n_rows),
        out_shape=(
            jax.ShapeDtypeStruct((block, depth), f32),
            jax.ShapeDtypeStruct((chunk, depth), f32),
        ),
        in_specs=[pl.BlockSpec(memory_space=pltpu.HBM)] * 3,
        out_specs=(pl.BlockSpec(memory_space=pltpu.VMEM),) * 2,
        scratch_shapes=[
            vmem((n_protos, block, depth), bf16),
            vmem((n_protos, block, depth), bf16),
            vmem((protos, depth), bf16),
            vmem((rows, protos), f32),
            vmem((rows, protos), f32),
            vmem((depth, rows), bf16),
            vmem((rows, LANES), f32),
            vmem((rows, LANES), f32),
            vmem((rows, LANES), f32),
            vmem((8, protos), f32),
            vmem((PASSES, 2, n_rows, 1, protos // 2), f32),
            vmem((1, protos), f32),
            vmem((PASSES, 2, n_protos, 1, rows // 2), f32),
            vmem((n_protos, 1, rows), f32),
            vmem((protos, depth), bf16),
            vmem((block, depth), bf16),
            vmem((block, depth), bf16),
            vmem((rows, protos), bf16),
            vmem((n_protos, block, depth), bf16),
            vmem((depth_z, LINES - 1, block, depth), bf16),
            vmem((depth_z, block, depth), bf16),
            vmem((depth_z, block, depth), bf16),
            vmem((4, 2, depth, half), bf16),
            vmem((4, 2, depth, half), bf16),
            vmem((3, 2, depth, half), bf16),
            vmem((2, depth, half), bf16),
            vmem((2, 2, depth, half), bf16),
            vmem((2, depth, half), f32),
            vmem((2, depth, half), f32),
            dma((3,)), dma, dma((depth_z - 1,)), dma((LINES - 1,)),
            dma, dma((depth_z - 1,)), dma((LINES - 1,)),
            dma((PASSES, 2)), dma((PASSES, 2)), dma((PASSES, 2)), dma((PASSES, 2)),
            dma, dma,
            dma((4,)), dma((4,)),
            dma((3, 2)), dma((2,)), dma((2, 2)),
            dma, dma((depth_z,)), dma, dma,
        ],
        compiler_params=pltpu.CompilerParams(
            collective_id=0, has_side_effects=True, vmem_limit_bytes=42 * 1024 * 1024
        ),
        name="head_step",
    )(*(pltpu.with_memory_space_constraint(v, pltpu.HBM) for v in (teacher_features, student_features, prototypes)))
    feature_grad, proto_grad = pl.pallas_call(
        store,
        out_shape=(
            jax.ShapeDtypeStruct((block, depth), f32),
            jax.ShapeDtypeStruct((chunk, depth), f32),
        ),
        in_specs=[pl.BlockSpec(memory_space=pltpu.VMEM)] * 2,
        out_specs=(pl.BlockSpec(memory_space=pl.ANY),) * 2,
        scratch_shapes=[dma, dma],
        compiler_params=pltpu.CompilerParams(vmem_limit_bytes=4 * 1024 * 1024),
        name="store",
    )(feature_grad, proto_grad)
    return feature_grad, proto_grad[None]


def solution(mesh):
    return jax.shard_map(
        on_device,
        mesh=mesh,
        in_specs=(P(("rows", "protos"), None), P(("rows", "protos"), None), P("protos", None)),
        out_specs=(P(("rows", "protos"), None), P("rows", "protos", None)),
        check_vma=False,
    )
```

```python
import functools
import math

import jax
import jax.numpy as jnp
from jax import lax
from jax.experimental import pallas as pl
from jax.experimental.pallas import tpu as pltpu
from jax.sharding import PartitionSpec as P

K = 131072
PASSES = 3
EPS = 1e-06
LANES = 128
STEP = 256
WIDE = 1024
MIDDLE = 512
CHIPS = 4
LINES = 4
MESH = pl.DeviceIdType.MESH
f32 = jnp.float32
bf16 = jnp.bfloat16


def unitize(values):
    values = values.astype(f32)
    return (values * lax.rsqrt(jnp.sum(values * values, axis=1, keepdims=True) + EPS)).astype(bf16)


def kernel(
    n_rows, n_protos, factor_rows,
    t_hbm, s_hbm, w_ref, fg_ref, pg_ref,
    tg, sg, uw, km, pm, st, rb, qb, acc, cbuf, cvec, rbuf, qbuf,
    wv, t_ref, s_ref, dall, fsend, fline, fout, frecv, psend, precv, xsend, relay, xrecv, pown,
    in_sem, turn_sem, t_ss, tz_rs, ty_rs, s_ss, sz_rs, sy_rs, c_ss, c_rs, r_ss, r_rs, q_ss, q_rs,
    p_ss, p_rs, x_ss, l_rs, x_rs, f_ss, fy_rs, g_ss, f_rs,
):
    rows, protos = km.shape
    depth = uw.shape[1]
    block = t_ref.shape[0]
    chunk = protos // n_rows
    half = chunk // 2
    scale = 1.5 * math.sqrt(depth)
    power = scale * math.log2(math.e)
    factor = scale * K / factor_rows
    r = lax.axis_index("rows")
    p = lax.axis_index("protos")

    loads = [
        pltpu.make_async_copy(source, target, in_sem.at[k])
        for k, (source, target) in enumerate(((t_hbm, t_ref), (s_hbm, s_ref), (w_ref, wv)))
    ]
    barrier = pltpu.get_barrier_semaphore()

    depth_z = n_protos // LINES
    y, z = lax.div(p, depth_z), lax.rem(p, depth_z)
    x, core = lax.div(r, 2), lax.rem(r, 2)

    def spot(dy, dz):
        return lax.rem(y + dy, LINES) * depth_z + lax.rem(z + dz, depth_z)

    def far_first(j):
        return depth_z // 2 + lax.div(j + 1, 2) * (1 - 2 * lax.rem(j, 2))

    def remote(source, target, send_sem, recv_sem, to):
        pltpu.make_async_remote_copy(
            src_ref=source, dst_ref=target, send_sem=send_sem, recv_sem=recv_sem,
            device_id=to, device_id_type=MESH,
        ).start()

    def greet(to):
        pl.semaphore_signal(barrier, inc=1, device_id=to, device_id_type=MESH)

    def all_protos(visit):
        def one(j, _):
            for dy in (2, 1, 3, 0):
                visit(spot(dy, far_first(j)))
            return 0

        lax.fori_loop(0, depth_z - 1, one, 0)
        for dy in (2, 1, 3):
            visit(spot(dy, 0))

    def all_rows(visit):
        for ahead in (2, 1, 3):
            for other in range(2):
                visit(lax.rem(x + ahead, CHIPS) * 2 + lax.rem(core + other, 2))
        visit(x * 2 + 1 - core)

    for dz in range(1, depth_z):
        greet({"protos": spot(0, dz)})
    for dy in range(1, LINES):
        greet({"protos": lax.rem(y + dy, LINES) * depth_z + z})
    all_rows(lambda q: greet({"rows": q}))
    for copy in loads:
        copy.start()

    def drain(view, sem):
        pltpu.make_async_copy(view, view, sem).wait()

    for copy in loads[:2]:
        copy.wait()
    tg[p] = unitize(t_ref[...])
    sg[p] = unitize(s_ref[...])
    pl.semaphore_wait(barrier, depth_z + LINES + n_rows - 3)

    def along_z(buf, send_sem, recv_sem):
        for j in range(depth_z - 1):
            dz = depth_z // 2 + (j + 1) // 2 * (1 - 2 * (j % 2))
            remote(
                buf.at[p], buf.at[p], send_sem, recv_sem.at[dz - 1], {"protos": spot(0, dz)}
            )

    def along_y(buf, q, send_sem, recv_sem, distances):
        for dy in distances:
            to = lax.rem(y + dy, LINES) * depth_z + z
            remote(buf.at[q], buf.at[q], send_sem, recv_sem.at[dy - 1], {"protos": to})

    def pass_on(buf, send_sem, z_sem, y_sem):
        along_y(buf, p, send_sem, y_sem, (1, 3))
        for j in reversed(range(depth_z - 1)):
            dz = depth_z // 2 + (j + 1) // 2 * (1 - 2 * (j % 2))
            q = spot(0, depth_z - dz)
            drain(buf.at[q], z_sem.at[dz - 1])
            along_y(buf, q, send_sem, y_sem, (1, 3))
        for k in range(depth_z):
            along_y(buf, y * depth_z + k, send_sem, y_sem, (2,))

    def column_here(buf, dy, y_sem):
        line = lax.rem(y + LINES - dy, LINES) * depth_z
        drain(buf.at[pl.ds(line, depth_z)], y_sem.at[dy - 1])

    along_z(tg, t_ss, tz_rs)
    along_z(sg, s_ss, sz_rs)
    loads[2].wait()

    def unit_step(i, _):
        at = pl.ds(pl.multiple_of(i * STEP, STEP), STEP)
        uw[at, :] = unitize(wv[at, :])
        return 0

    lax.fori_loop(0, protos // STEP, unit_step, 0)

    others = pl.ds(0, n_protos - 1)
    pass_on(tg, t_ss, tz_rs, ty_rs)
    def logits(left, i, width):
        at = pl.ds(pl.multiple_of(i * width, width), width)
        values = lax.dot_general(
            left, uw[at, :], (((1,), (1,)), ((), ())), preferred_element_type=f32
        )
        return at, jnp.exp2(values * power)

    pair_rows = 2 * depth_z * block

    def kernel_half(pair, c, first):
        lines = pl.ds(pair * 2 * depth_z, 2 * depth_z)
        here = pl.ds(pl.multiple_of(pair * pair_rows, pair_rows), pair_rows)
        teacher = tg[lines].reshape(pair_rows, depth)
        steps = protos // 2 // WIDE

        def one(i, _):
            at, values = logits(teacher, c * steps + i, WIDE)
            km[here, at] = values
            part = jnp.sum(values, axis=0, keepdims=True)
            to = pl.ds(pl.multiple_of(i * WIDE, WIDE), WIDE)
            cbuf[0, c, r, :, to] = part if first else cbuf[0, c, r, :, to] + part
            return 0

        lax.fori_loop(0, steps, one, 0)

    odd = lax.rem(y, 2)
    near = 3 - 2 * odd
    line = lax.rem(y + LINES - near, LINES) * depth_z
    drain(tg.at[pl.ds(line, depth_z)], ty_rs.at[near - 1])
    kernel_half(lax.div(y, 2), 0, True)
    kernel_half(lax.div(y, 2), 1, True)
    pass_on(sg, s_ss, sz_rs, sy_rs)
    line = lax.rem(y + near, LINES) * depth_z
    drain(tg.at[pl.ds(line, depth_z)], ty_rs.at[LINES - near - 1])
    column_here(tg, 2, ty_rs)

    def column(values):
        return jnp.transpose(jnp.broadcast_to(values, (LANES, LANES)))

    def to_columns(values, ref):
        for g in range(rows // LANES):
            ref[g * LANES:(g + 1) * LANES, :] = column(values[:, g * LANES:(g + 1) * LANES])

    def lane_sums(acc, store, groups):
        for g in groups:
            turned = jnp.transpose(acc[g * LANES:(g + 1) * LANES, :])
            at = slice((g - groups[0]) * LANES, (g - groups[0] + 1) * LANES)
            store(at, jnp.sum(turned, axis=0, keepdims=True))

    tiles = protos // LANES
    groups = rows // LANES
    side = protos // 2

    def lane(j):
        return slice(j * LANES, (j + 1) * LANES)

    def rows_of(i):
        return pl.ds(pl.multiple_of(i * 8, 8), 8)

    def column_sweep(which):
        def one(i, sums):
            at = rows_of(i)
            value = rb[at, :]
            return tuple(s + km[at, lane(j)] * value for s, j in zip(sums, which))

        return lax.fori_loop(
            0, rows // 8, one, tuple(jnp.zeros((8, LANES), f32) for _ in which), unroll=4
        )

    def row_sweep(c):
        which = range(c * tiles // 2, (c + 1) * tiles // 2)
        cols = [jnp.broadcast_to(cvec[:, lane(j)], (8, LANES)) for j in which]

        def one(i, _):
            at = rows_of(i)
            parts = [km[at, lane(j)] * col for j, col in zip(which[:4], cols[:4])]
            for k in range(4, len(which)):
                parts[k % 4] = parts[k % 4] + km[at, lane(which[k])] * cols[k]
            total = (parts[0] + parts[1]) + (parts[2] + parts[3])
            acc[at, :] = total if c == 0 else acc[at, :] + total
            return 0

        lax.fori_loop(0, rows // 8, one, 0, unroll=4)

    def send_columns(step, c):
        mine = cbuf.at[step, c, r]
        sems = c_ss.at[step, c], c_rs.at[step, c]
        all_rows(lambda q: remote(mine, mine, *sems, {"rows": q}))

    def send_sums(step):
        mine = rbuf.at[step, p]
        sems = r_ss.at[step], r_rs.at[step]
        all_protos(lambda q: remote(mine, mine, *sems, {"protos": q}))

    def take_columns(step, c):
        drain(cbuf.at[step, c, pl.ds(0, n_rows - 1)], c_rs.at[step, c])
        cvec[:, c * side:(c + 1) * side] = 1.0 / jnp.sum(cbuf[step, c], axis=0)

    def take_sums(step):
        drain(rbuf.at[step, others], r_rs.at[step])
        to_columns(1.0 / jnp.sum(rbuf[step], axis=0), rb)

    def column_pass(step):
        take_sums(step - 1)
        for c in range(2):
            which = range(c * tiles // 2, (c + 1) * tiles // 2)
            for j, value in zip(which, column_sweep(which)):
                value = jnp.sum(value, axis=0, keepdims=True)
                cbuf[step, c, r, :, lane(j - which[0])] = value
            send_columns(step, c)

    def row_pass(step):
        for c in range(2):
            take_columns(step, c)
            row_sweep(c)

        def store(at, value):
            rbuf[step, p, :, at] = value

        lane_sums(acc, store, range(groups))
        send_sums(step)

    steps = protos // MIDDLE

    def student(begin, end):
        units = sg[...].reshape(rows, depth)

        def one(i, _):
            at, values = logits(units, i, MIDDLE)
            pm[:, at] = values
            qb[...] += sum(values[:, j * LANES:(j + 1) * LANES] for j in range(MIDDLE // LANES))
            return 0

        lax.fori_loop(begin, end, one, 0)

    def student_begin():
        for dy in (1, 2, 3):
            column_here(sg, dy, sy_rs)
        qb[...] = jnp.zeros_like(qb)
        student(0, steps // 2)

    def student_end():
        student(steps // 2, steps)

        def store(at, value):
            qbuf[p, :, at] = value

        lane_sums(qb, store, range(groups))
        all_protos(lambda q: remote(qbuf.at[p], qbuf.at[p], q_ss, q_rs, {"protos": q}))

    for c in range(2):
        kernel_half(1 - lax.div(y, 2), c, False)
        send_columns(0, c)

    chips = [lax.rem(x + ahead, CHIPS) for ahead in (2, 1, 3, 0)]
    places = [(0, 1), (0, 0), (1, 1), (2, 1), (1, 0), (2, 0), (3, 1), (3, 0)]
    owners = [chips[k] * 2 + lax.rem(core + other, 2) for k, other in places]

    def chunk_of(place):
        return pl.ds(pl.multiple_of(owners[place] * chunk, chunk), chunk)

    turns = [
        pltpu.make_async_copy(
            uw.at[chunk_of(k)], wv.at[pl.ds(k * chunk, chunk)], turn_sem.at[k]
        )
        for k in range(n_rows)
    ]

    for step in range(PASSES):
        if step > 0:
            column_pass(step)
        if step == 1:
            student_end()
        elif step == 2:
            drain(qbuf.at[others], q_rs)
            to_columns(1.0 / jnp.sum(qbuf[...], axis=0), qb)
        row_pass(step)
        if step == 0:
            student_begin()
        elif step == 1:
            for copy in turns:
                copy.start()
            st[...] = jnp.transpose(sg[...].reshape(rows, depth).astype(f32)).astype(bf16)
    take_sums(PASSES - 1)

    def send(source, target, send_sem, recv_sem, to):
        remote(source, target, send_sem, recv_sem, {"rows": to})

    up = lax.rem(x + 1, CHIPS) * 2 + core
    down = lax.rem(x + CHIPS - 1, CHIPS) * 2 + core
    mate = x * 2 + 1 - core

    def delta(place):
        at = chunk_of(place)
        to = slice(place * chunk, (place + 1) * chunk)
        cols = cvec[:, at]
        for i in range(rows // 16):
            here = slice(i * 16, (i + 1) * 16)
            row = jnp.concatenate([rb[here, :]] * (chunk // LANES), axis=1)
            inv = jnp.concatenate([qb[here, :]] * (chunk // LANES), axis=1)
            value = pm[here, at] * inv - km[here, at] * row * cols
            dall[here, to] = value.astype(bf16)

    def term(place, following=None):
        part = jnp.dot(
            st[...], dall[:, place * chunk:(place + 1) * chunk], preferred_element_type=f32
        )
        if following is not None:
            delta(following)
        k, other = places[place]
        if other:
            psend[k, 0] = part[:, :half].astype(bf16)
            psend[k, 1] = part[:, half:].astype(bf16)
            for h in range(2):
                send(psend.at[k, h], precv.at[k, h], p_ss.at[k, h], p_rs.at[k, h], mate)
        else:
            pown[k, 0] = part[:, :half]
            pown[k, 1] = part[:, half:]

    def joined(k, h):
        return pown[k, h] + precv[k, h].astype(f32)

    def features():
        half_rows = rows // 2

        def one(i, _):
            here = pl.ds(pl.multiple_of(i * half_rows, half_rows), half_rows)
            part = jnp.dot(dall[here, :], wv[...], preferred_element_type=f32).astype(bf16)
            to = pl.ds(i * (n_protos // 2), n_protos // 2)
            fsend[to] = part.reshape(n_protos // 2, block, depth)
            return 0

        lax.fori_loop(0, 2, one, 0)

        def post(j, _):
            dz = far_first(j)
            for dy in (2, 1, 3):
                q = spot(dy, dz)
                to = lax.rem(y + dy, LINES) * depth_z + z
                remote(fsend.at[q], fline.at[j, dy - 1], f_ss, fy_rs.at[j], {"protos": to})
            return 0

        lax.fori_loop(0, depth_z, post, 0)

    def features_on():
        def one(j, _):
            q = spot(0, far_first(j))
            drain(fline.at[j], fy_rs.at[j])
            value = fsend[q].astype(f32) + fline[j, 0].astype(f32)
            value = value + (fline[j, 1].astype(f32) + fline[j, 2].astype(f32))
            fout[j] = value.astype(bf16)
            return 0

        def step(j, _):
            one(j, 0)
            q = spot(0, far_first(j))
            remote(fout.at[j], frecv.at[z], g_ss, f_rs, {"protos": q})
            return 0

        lax.fori_loop(0, depth_z - 1, step, 0)
        one(depth_z - 1, 0)
        frecv[z] = fout[depth_z - 1]

    delta(0)
    for h in range(2):
        part = jnp.dot(
            st[...], dall[:, h * half:(h + 1) * half], preferred_element_type=f32
        )
        psend[0, h] = part.astype(bf16)
        send(psend.at[0, h], precv.at[0, h], p_ss.at[0, h], p_rs.at[0, h], mate)
        if h == 0:
            delta(1)
    term(1, 2)
    term(2, 3)
    for h, to in ((0, up), (1, down)):
        drain(precv.at[0, h], p_rs.at[0, h])
        xsend[0, h] = joined(0, h).astype(bf16)
        send(xsend.at[0, h], relay.at[h], x_ss.at[0, h], l_rs.at[h], to)
        if h == 0:
            term(3, 4)
    term(4, 5)
    term(5, 6)
    for k, h, to in ((1, 1, up), (2, 0, down)):
        drain(precv.at[k, h], p_rs.at[k, h])
        xsend[k, h] = joined(k, h).astype(bf16)
        send(xsend.at[k, h], xrecv.at[k - 1, h], x_ss.at[k, h], x_rs.at[k - 1, h], to)
    term(6, 7)
    for copy in turns:
        copy.wait()
    features()
    term(7)
    for k, h, to in ((1, 0, up), (2, 1, down)):
        drain(precv.at[k, h], p_rs.at[k, h])
        drain(relay.at[h], l_rs.at[h])
        xsend[k, h] = (joined(k, h) + relay[h].astype(f32)).astype(bf16)
        send(xsend.at[k, h], xrecv.at[k - 1, h], x_ss.at[k, h], x_rs.at[k - 1, h], to)

    features_on()
    drain(frecv.at[pl.ds(0, depth_z - 1)], f_rs)
    total = jnp.zeros((block, depth), f32)
    total = lax.fori_loop(0, depth_z, lambda i, a: a + frecv[i].astype(f32), total)
    fg_ref[...] = scale * total

    for h in range(2):
        drain(precv.at[3, h], p_rs.at[3, h])
    for side in range(2):
        for h in range(2):
            drain(xrecv.at[side, h], x_rs.at[side, h])
    for h in range(2):
        whole = joined(3, h) + xrecv[0, h].astype(f32) + xrecv[1, h].astype(f32)
        pg_ref[h * half:(h + 1) * half, :] = jnp.transpose(factor * whole)

    drain(tg.at[others], t_ss)
    drain(sg.at[others], s_ss)
    drain(qbuf.at[others], q_ss)
    drain(fline, f_ss)
    drain(frecv.at[pl.ds(0, depth_z - 1)], g_ss)
    for step in range(PASSES):
        for h in range(2):
            drain(cbuf.at[step, h, pl.ds(0, n_rows - 1)], c_ss.at[step, h])
        drain(rbuf.at[step, others], r_ss.at[step])
    for k in range(4):
        for h in range(2):
            drain(psend.at[k, h], p_ss.at[k, h])
    for k in range(3):
        for h in range(2):
            drain(xsend.at[k, h], x_ss.at[k, h])


def store(feature, proto, feature_out, proto_out, f_sem, p_sem):
    copies = [
        pltpu.make_async_copy(proto, proto_out, p_sem),
        pltpu.make_async_copy(feature, feature_out, f_sem),
    ]
    for copy in copies:
        copy.start()
    for copy in copies:
        copy.wait()


def on_device(teacher_features, student_features, prototypes):
    n_rows, n_protos = lax.axis_size("rows"), lax.axis_size("protos")
    block, depth = teacher_features.shape
    protos = prototypes.shape[0]
    rows = block * n_protos
    chunk = protos // n_rows
    half = chunk // 2
    depth_z = n_protos // LINES
    dma = pltpu.SemaphoreType.DMA
    vmem = pltpu.VMEM
    feature_grad, proto_grad = pl.pallas_call(
        functools.partial(kernel, n_rows, n_protos, rows * n_rows),
        out_shape=(
            jax.ShapeDtypeStruct((block, depth), f32),
            jax.ShapeDtypeStruct((chunk, depth), f32),
        ),
        in_specs=[pl.BlockSpec(memory_space=pltpu.HBM)] * 3,
        out_specs=(pl.BlockSpec(memory_space=pltpu.VMEM),) * 2,
        scratch_shapes=[
            vmem((n_protos, block, depth), bf16),
            vmem((n_protos, block, depth), bf16),
            vmem((protos, depth), bf16),
            vmem((rows, protos), f32),
            vmem((rows, protos), f32),
            vmem((depth, rows), bf16),
            vmem((rows, LANES), f32),
            vmem((rows, LANES), f32),
            vmem((rows, LANES), f32),
            vmem((PASSES, 2, n_rows, 1, protos // 2), f32),
            vmem((1, protos), f32),
            vmem((PASSES, n_protos, 1, rows), f32),
            vmem((n_protos, 1, rows), f32),
            vmem((protos, depth), bf16),
            vmem((block, depth), bf16),
            vmem((block, depth), bf16),
            vmem((rows, protos), bf16),
            vmem((n_protos, block, depth), bf16),
            vmem((depth_z, LINES - 1, block, depth), bf16),
            vmem((depth_z, block, depth), bf16),
            vmem((depth_z, block, depth), bf16),
            vmem((4, 2, depth, half), bf16),
            vmem((4, 2, depth, half), bf16),
            vmem((3, 2, depth, half), bf16),
            vmem((2, depth, half), bf16),
            vmem((2, 2, depth, half), bf16),
            vmem((4, 2, depth, half), f32),
            dma((3,)), dma((n_rows,)), dma, dma((depth_z - 1,)), dma((LINES - 1,)),
            dma, dma((depth_z - 1,)), dma((LINES - 1,)),
            dma((PASSES, 2)), dma((PASSES, 2)), dma((PASSES,)), dma((PASSES,)),
            dma, dma,
            dma((4, 2)), dma((4, 2)),
            dma((3, 2)), dma((2,)), dma((2, 2)),
            dma, dma((depth_z,)), dma, dma,
        ],
        compiler_params=pltpu.CompilerParams(
            collective_id=0, has_side_effects=True, vmem_limit_bytes=46 * 1024 * 1024
        ),
        name="head_step",
    )(*(pltpu.with_memory_space_constraint(v, pltpu.HBM) for v in (teacher_features, student_features, prototypes)))
    feature_grad, proto_grad = pl.pallas_call(
        store,
        out_shape=(
            jax.ShapeDtypeStruct((block, depth), f32),
            jax.ShapeDtypeStruct((chunk, depth), f32),
        ),
        in_specs=[pl.BlockSpec(memory_space=pltpu.VMEM)] * 2,
        out_specs=(pl.BlockSpec(memory_space=pl.ANY),) * 2,
        scratch_shapes=[dma, dma],
        compiler_params=pltpu.CompilerParams(vmem_limit_bytes=4 * 1024 * 1024),
        name="store",
    )(feature_grad, proto_grad)
    return feature_grad, proto_grad[None]


def solution(mesh):
    return jax.shard_map(
        on_device,
        mesh=mesh,
        in_specs=(P(("rows", "protos"), None), P(("rows", "protos"), None), P("protos", None)),
        out_specs=(P(("rows", "protos"), None), P("rows", "protos", None)),
        check_vma=False,
    )
```

```python
import functools
import math

import jax
import jax.numpy as jnp
from jax import lax
from jax.experimental import pallas as pl
from jax.experimental.pallas import tpu as pltpu
from jax.sharding import PartitionSpec as P

K = 131072
PASSES = 3
EPS = 1e-06
LANES = 128
STEP = 256
WIDE = 2048
MIDDLE = 512
CHIPS = 4
LINES = 4
MESH = pl.DeviceIdType.MESH
f32 = jnp.float32
bf16 = jnp.bfloat16


def unitize(values):
    values = values.astype(f32)
    return (values * lax.rsqrt(jnp.sum(values * values, axis=1, keepdims=True) + EPS)).astype(bf16)


def kernel(
    n_rows, n_protos, factor_rows,
    t_hbm, s_hbm, w_ref, fg_ref, pg_ref,
    tg, sg, uw, km, pm, st, rb, qb, acc, cbuf, cvec, rbuf, qbuf,
    wv, t_ref, s_ref, dall, fsend, fline, fout, frecv, psend, precv, xsend, xnear, relay, xrecv, pown,
    in_sem, turn_sem, t_ss, tz_rs, ty_rs, s_ss, sz_rs, sy_rs, c_ss, c_rs, r_ss, r_rs, q_ss, q_rs,
    p_ss, p_rs, x_ss, l_rs, x_rs, f_ss, fy_rs, g_ss, f_rs,
):
    rows, protos = km.shape
    depth = uw.shape[1]
    block = t_ref.shape[0]
    chunk = protos // n_rows
    half = chunk // 2
    scale = 1.5 * math.sqrt(depth)
    power = scale * math.log2(math.e)
    factor = scale * K / factor_rows
    r = lax.axis_index("rows")
    p = lax.axis_index("protos")

    loads = [
        pltpu.make_async_copy(source, target, in_sem.at[k])
        for k, (source, target) in enumerate(((t_hbm, t_ref), (s_hbm, s_ref), (w_ref, wv)))
    ]
    barrier = pltpu.get_barrier_semaphore()

    depth_z = n_protos // LINES
    y, z = lax.div(p, depth_z), lax.rem(p, depth_z)
    x, core = lax.div(r, 2), lax.rem(r, 2)

    def spot(dy, dz):
        return lax.rem(y + dy, LINES) * depth_z + lax.rem(z + dz, depth_z)

    def far_first(j):
        return depth_z // 2 + lax.div(j + 1, 2) * (1 - 2 * lax.rem(j, 2))

    def remote(source, target, send_sem, recv_sem, to):
        pltpu.make_async_remote_copy(
            src_ref=source, dst_ref=target, send_sem=send_sem, recv_sem=recv_sem,
            device_id=to, device_id_type=MESH,
        ).start()

    def greet(to):
        pl.semaphore_signal(barrier, inc=1, device_id=to, device_id_type=MESH)

    def all_protos(visit):
        def one(j, _):
            for dy in (2, 1, 3, 0):
                visit(spot(dy, far_first(j)))
            return 0

        lax.fori_loop(0, depth_z - 1, one, 0)
        for dy in (2, 1, 3):
            visit(spot(dy, 0))

    def all_rows(visit):
        for ahead in (2, 1, 3):
            for other in range(2):
                visit(lax.rem(x + ahead, CHIPS) * 2 + lax.rem(core + other, 2))
        visit(x * 2 + 1 - core)

    for dz in range(1, depth_z):
        greet({"protos": spot(0, dz)})
    for dy in range(1, LINES):
        greet({"protos": lax.rem(y + dy, LINES) * depth_z + z})
    all_rows(lambda q: greet({"rows": q}))
    for copy in loads:
        copy.start()

    def drain(view, sem):
        pltpu.make_async_copy(view, view, sem).wait()

    for copy in loads[:2]:
        copy.wait()
    tg[p] = unitize(t_ref[...])
    sg[p] = unitize(s_ref[...])
    pl.semaphore_wait(barrier, depth_z + LINES + n_rows - 3)

    def along_z(buf, send_sem, recv_sem):
        for j in reversed(range(depth_z - 1)):
            dz = depth_z // 2 + (j + 1) // 2 * (1 - 2 * (j % 2))
            remote(
                buf.at[p], buf.at[p], send_sem, recv_sem.at[dz - 1], {"protos": spot(0, dz)}
            )

    def along_y(buf, q, send_sem, recv_sem, distances):
        for dy in distances:
            to = lax.rem(y + dy, LINES) * depth_z + z
            remote(buf.at[q], buf.at[q], send_sem, recv_sem.at[dy - 1], {"protos": to})

    def pass_on(buf, send_sem, z_sem, y_sem):
        for j in reversed(range(depth_z - 1)):
            dz = depth_z // 2 + (j + 1) // 2 * (1 - 2 * (j % 2))
            q = spot(0, depth_z - dz)
            drain(buf.at[q], z_sem.at[dz - 1])
            along_y(buf, q, send_sem, y_sem, (1, 3, 2))

    def column_here(buf, dy, y_sem):
        line = lax.rem(y + LINES - dy, LINES) * depth_z
        drain(buf.at[pl.ds(line, depth_z)], y_sem.at[dy - 1])

    along_z(tg, t_ss, tz_rs)
    along_y(tg, p, t_ss, ty_rs, (1, 3, 2))
    along_z(sg, s_ss, sz_rs)
    loads[2].wait()

    def unit_step(i, _):
        at = pl.ds(pl.multiple_of(i * STEP, STEP), STEP)
        uw[at, :] = unitize(wv[at, :])
        return 0

    lax.fori_loop(0, protos // STEP, unit_step, 0)

    others = pl.ds(0, n_protos - 1)
    pass_on(tg, t_ss, tz_rs, ty_rs)
    def logits(left, i, width):
        at = pl.ds(pl.multiple_of(i * width, width), width)
        values = lax.dot_general(
            left, uw[at, :], (((1,), (1,)), ((), ())), preferred_element_type=f32
        )
        return at, jnp.exp2(values * power)

    pair_rows = 2 * depth_z * block

    def kernel_half(pair, c, first):
        lines = pl.ds(pair * 2 * depth_z, 2 * depth_z)
        here = pl.ds(pl.multiple_of(pair * pair_rows, pair_rows), pair_rows)
        teacher = tg[lines].reshape(pair_rows, depth)
        steps = protos // 2 // WIDE

        def one(i, _):
            at, values = logits(teacher, c * steps + i, WIDE)
            km[here, at] = values
            part = jnp.sum(values, axis=0, keepdims=True)
            to = pl.ds(pl.multiple_of(i * WIDE, WIDE), WIDE)
            cbuf[0, c, r, :, to] = part if first else cbuf[0, c, r, :, to] + part
            return 0

        lax.fori_loop(0, steps, one, 0)

    odd = lax.rem(y, 2)
    near = 3 - 2 * odd
    line = lax.rem(y + LINES - near, LINES) * depth_z
    drain(tg.at[pl.ds(line, depth_z)], ty_rs.at[near - 1])
    kernel_half(lax.div(y, 2), 0, True)
    kernel_half(lax.div(y, 2), 1, True)
    along_y(sg, p, s_ss, sy_rs, (1, 3, 2))
    pass_on(sg, s_ss, sz_rs, sy_rs)
    line = lax.rem(y + near, LINES) * depth_z
    drain(tg.at[pl.ds(line, depth_z)], ty_rs.at[LINES - near - 1])
    column_here(tg, 2, ty_rs)

    def column(values):
        return jnp.transpose(jnp.broadcast_to(values, (LANES, LANES)))

    def to_columns(values, ref):
        for g in range(rows // LANES):
            ref[g * LANES:(g + 1) * LANES, :] = column(values[:, g * LANES:(g + 1) * LANES])

    def lane_sums(acc, store, groups):
        for g in groups:
            turned = jnp.transpose(acc[g * LANES:(g + 1) * LANES, :])
            at = slice((g - groups[0]) * LANES, (g - groups[0] + 1) * LANES)
            store(at, jnp.sum(turned, axis=0, keepdims=True))

    tiles = protos // LANES
    groups = rows // LANES
    side = protos // 2

    def lane(j):
        return slice(j * LANES, (j + 1) * LANES)

    def rows_of(i):
        return pl.ds(pl.multiple_of(i * 8, 8), 8)

    def column_sweep(which):
        def one(i, sums):
            at = rows_of(i)
            value = rb[at, :]
            return tuple(s + km[at, lane(j)] * value for s, j in zip(sums, which))

        return lax.fori_loop(
            0, rows // 8, one, tuple(jnp.zeros((8, LANES), f32) for _ in which), unroll=4
        )

    def row_sweep(c):
        which = range(c * tiles // 2, (c + 1) * tiles // 2)
        cols = [jnp.broadcast_to(cvec[:, lane(j)], (8, LANES)) for j in which]

        def one(i, _):
            at = rows_of(i)
            parts = [km[at, lane(j)] * col for j, col in zip(which[:4], cols[:4])]
            for k in range(4, len(which)):
                parts[k % 4] = parts[k % 4] + km[at, lane(which[k])] * cols[k]
            total = (parts[0] + parts[1]) + (parts[2] + parts[3])
            acc[at, :] = total if c == 0 else acc[at, :] + total
            return 0

        lax.fori_loop(0, rows // 8, one, 0, unroll=4)

    def scale_both():
        cols = [jnp.broadcast_to(cvec[:, lane(j)], (8, LANES)) for j in range(tiles)]

        def one(i, _):
            at = rows_of(i)
            value = qb[at, :]
            for j in range(tiles):
                pm[at, lane(j)] = pm[at, lane(j)] * value
                km[at, lane(j)] = km[at, lane(j)] * cols[j]
            return 0

        lax.fori_loop(0, rows // 8, one, 0, unroll=2)

    def send_columns(step, c):
        mine = cbuf.at[step, c, r]
        sems = c_ss.at[step, c], c_rs.at[step, c]
        all_rows(lambda q: remote(mine, mine, *sems, {"rows": q}))

    def send_sums(step):
        mine = rbuf.at[step, p]
        sems = r_ss.at[step], r_rs.at[step]
        all_protos(lambda q: remote(mine, mine, *sems, {"protos": q}))

    def take_columns(step, c):
        drain(cbuf.at[step, c, pl.ds(0, n_rows - 1)], c_rs.at[step, c])
        cvec[:, c * side:(c + 1) * side] = 1.0 / jnp.sum(cbuf[step, c], axis=0)

    def take_sums(step):
        drain(rbuf.at[step, others], r_rs.at[step])
        to_columns(1.0 / jnp.sum(rbuf[step], axis=0), rb)

    def column_pass(step):
        take_sums(step - 1)
        for c in range(2):
            which = range(c * tiles // 2, (c + 1) * tiles // 2)
            for j, value in zip(which, column_sweep(which)):
                value = jnp.sum(value, axis=0, keepdims=True)
                cbuf[step, c, r, :, lane(j - which[0])] = value
            send_columns(step, c)

    def row_pass(step):
        for c in range(2):
            take_columns(step, c)
            row_sweep(c)

        def store(at, value):
            rbuf[step, p, :, at] = value

        lane_sums(acc, store, range(groups))
        send_sums(step)

    steps = protos // MIDDLE

    def student(begin, end):
        units = sg[...].reshape(rows, depth)

        def one(i, _):
            at, values = logits(units, i, MIDDLE)
            pm[:, at] = values
            qb[...] += sum(values[:, j * LANES:(j + 1) * LANES] for j in range(MIDDLE // LANES))
            return 0

        lax.fori_loop(begin, end, one, 0)

    def student_begin():
        for dy in (1, 2, 3):
            column_here(sg, dy, sy_rs)
        qb[...] = jnp.zeros_like(qb)
        student(0, steps // 2)

    def student_end():
        student(steps // 2, steps)

        def store(at, value):
            qbuf[p, :, at] = value

        lane_sums(qb, store, range(groups))
        all_protos(lambda q: remote(qbuf.at[p], qbuf.at[p], q_ss, q_rs, {"protos": q}))

    for c in range(2):
        kernel_half(1 - lax.div(y, 2), c, False)
        send_columns(0, c)

    chips = [lax.rem(x + ahead, CHIPS) for ahead in (2, 1, 3, 0)]
    places = [(0, 1), (0, 0), (1, 1), (2, 1), (1, 0), (2, 0), (3, 1), (3, 0)]
    owners = [chips[k] * 2 + lax.rem(core + other, 2) for k, other in places]

    def chunk_of(place):
        return pl.ds(pl.multiple_of(owners[place] * chunk, chunk), chunk)

    turns = [
        pltpu.make_async_copy(
            uw.at[chunk_of(k)], wv.at[pl.ds(k * chunk, chunk)], turn_sem.at[k]
        )
        for k in range(n_rows)
    ]

    for step in range(PASSES):
        if step > 0:
            column_pass(step)
        if step == 1:
            student_end()
        elif step == 2:
            drain(qbuf.at[others], q_rs)
            to_columns(1.0 / jnp.sum(qbuf[...], axis=0), qb)
        row_pass(step)
        if step == 0:
            student_begin()
        elif step == 1:
            for copy in turns:
                copy.start()
            st[...] = jnp.transpose(sg[...].reshape(rows, depth).astype(f32)).astype(bf16)
    scale_both()
    take_sums(PASSES - 1)

    def send(source, target, send_sem, recv_sem, to):
        remote(source, target, send_sem, recv_sem, {"rows": to})

    up = lax.rem(x + 1, CHIPS) * 2 + core
    down = lax.rem(x + CHIPS - 1, CHIPS) * 2 + core
    mate = x * 2 + 1 - core

    def delta(place):
        at = chunk_of(place)
        to = slice(place * chunk, (place + 1) * chunk)
        for i in range(rows // 16):
            here = slice(i * 16, (i + 1) * 16)
            row = jnp.concatenate([rb[here, :]] * (chunk // LANES), axis=1)
            value = pm[here, at] - km[here, at] * row
            dall[here, to] = value.astype(bf16)

    def term(place, following=None):
        part = jnp.dot(
            st[...], dall[:, place * chunk:(place + 1) * chunk], preferred_element_type=f32
        )
        if following is not None:
            delta(following)
        k, other = places[place]
        if other:
            psend[k, 0] = part[:, :half].astype(bf16)
            psend[k, 1] = part[:, half:].astype(bf16)
            for h in range(2):
                send(psend.at[k, h], precv.at[k, h], p_ss.at[k, h], p_rs.at[k, h], mate)
        else:
            pown[k, 0] = part[:, :half]
            pown[k, 1] = part[:, half:]

    def joined(k, h):
        return pown[k, h] + precv[k, h].astype(f32)

    def features():
        half_rows = rows // 2

        def one(i, _):
            here = pl.ds(pl.multiple_of(i * half_rows, half_rows), half_rows)
            part = jnp.dot(dall[here, :], wv[...], preferred_element_type=f32).astype(bf16)
            to = pl.ds(i * (n_protos // 2), n_protos // 2)
            fsend[to] = part.reshape(n_protos // 2, block, depth)
            return 0

        lax.fori_loop(0, 2, one, 0)

        def post(j, _):
            dz = far_first(j)
            for dy in (2, 1, 3):
                q = spot(dy, dz)
                to = lax.rem(y + dy, LINES) * depth_z + z
                remote(fsend.at[q], fline.at[j, dy - 1], f_ss, fy_rs.at[j], {"protos": to})
            return 0

        lax.fori_loop(0, depth_z, post, 0)

    def features_on():
        def one(j, _):
            q = spot(0, far_first(j))
            drain(fline.at[j], fy_rs.at[j])
            value = fsend[q].astype(f32) + fline[j, 0].astype(f32)
            value = value + (fline[j, 1].astype(f32) + fline[j, 2].astype(f32))
            fout[j] = value.astype(bf16)
            return 0

        def step(j, _):
            one(j, 0)
            q = spot(0, far_first(j))
            remote(fout.at[j], frecv.at[z], g_ss, f_rs, {"protos": q})
            return 0

        lax.fori_loop(0, depth_z - 1, step, 0)
        one(depth_z - 1, 0)
        frecv[z] = fout[depth_z - 1]

    delta(0)
    for h in range(2):
        part = jnp.dot(
            st[...], dall[:, h * half:(h + 1) * half], preferred_element_type=f32
        )
        psend[0, h] = part.astype(bf16)
        send(psend.at[0, h], precv.at[0, h], p_ss.at[0, h], p_rs.at[0, h], mate)
        if h == 0:
            delta(1)
    term(1, 2)
    term(2, 3)
    for h, to in ((0, up), (1, down)):
        drain(precv.at[0, h], p_rs.at[0, h])
        xsend[h] = joined(0, h).astype(bf16)
        send(xsend.at[h], relay.at[h], x_ss.at[0, h], l_rs.at[h], to)
        if h == 0:
            term(3, 4)
    term(4, 5)
    term(5, 6)
    for k, h, to in ((1, 1, up), (2, 0, down)):
        drain(precv.at[k, h], p_rs.at[k, h])
        xnear[k - 1, h] = jnp.transpose(joined(k, h)).astype(bf16)
        send(xnear.at[k - 1, h], xrecv.at[k - 1, h], x_ss.at[k, h], x_rs.at[k - 1, h], to)
    term(6, 7)
    for copy in turns:
        copy.wait()
    features()
    term(7)
    for k, h, to in ((1, 0, up), (2, 1, down)):
        drain(precv.at[k, h], p_rs.at[k, h])
        drain(relay.at[h], l_rs.at[h])
        xnear[k - 1, h] = jnp.transpose(joined(k, h) + relay[h].astype(f32)).astype(bf16)
        send(xnear.at[k - 1, h], xrecv.at[k - 1, h], x_ss.at[k, h], x_rs.at[k - 1, h], to)

    features_on()
    for h in range(2):
        drain(precv.at[3, h], p_rs.at[3, h])
        pg_ref[h * half:(h + 1) * half, :] = jnp.transpose(joined(3, h))

    drain(tg.at[others], t_ss)
    drain(sg.at[others], s_ss)
    drain(qbuf.at[others], q_ss)
    for step in range(PASSES):
        for h in range(2):
            drain(cbuf.at[step, h, pl.ds(0, n_rows - 1)], c_ss.at[step, h])
        drain(rbuf.at[step, others], r_ss.at[step])
    for h in range(2):
        for k in range(4):
            drain(psend.at[k, h], p_ss.at[k, h])
        drain(xsend.at[h], x_ss.at[0, h])
    drain(fline, f_ss)

    drain(frecv.at[pl.ds(0, depth_z - 1)], f_rs)
    total = jnp.zeros((block, depth), f32)
    total = lax.fori_loop(0, depth_z, lambda i, a: a + frecv[i].astype(f32), total)
    fg_ref[...] = scale * total
    drain(frecv.at[pl.ds(0, depth_z - 1)], g_ss)

    for h in range(2):
        for line in range(2):
            drain(xrecv.at[line, h], x_rs.at[line, h])
    here = slice(0, chunk)
    received = [xrecv[line].reshape(chunk, depth).astype(f32) for line in range(2)]
    pg_ref[here, :] = factor * (pg_ref[here, :] + (received[0] + received[1]))
    for k in range(2):
        for h in range(2):
            drain(xnear.at[k, h], x_ss.at[k + 1, h])


def store(feature, proto, feature_out, proto_out, f_sem, p_sem):
    copies = [
        pltpu.make_async_copy(proto, proto_out, p_sem),
        pltpu.make_async_copy(feature, feature_out, f_sem),
    ]
    for copy in copies:
        copy.start()
    for copy in copies:
        copy.wait()


def on_device(teacher_features, student_features, prototypes):
    n_rows, n_protos = lax.axis_size("rows"), lax.axis_size("protos")
    block, depth = teacher_features.shape
    protos = prototypes.shape[0]
    rows = block * n_protos
    chunk = protos // n_rows
    half = chunk // 2
    depth_z = n_protos // LINES
    dma = pltpu.SemaphoreType.DMA
    vmem = pltpu.VMEM
    feature_grad, proto_grad = pl.pallas_call(
        functools.partial(kernel, n_rows, n_protos, rows * n_rows),
        out_shape=(
            jax.ShapeDtypeStruct((block, depth), f32),
            jax.ShapeDtypeStruct((chunk, depth), f32),
        ),
        in_specs=[pl.BlockSpec(memory_space=pltpu.HBM)] * 3,
        out_specs=(pl.BlockSpec(memory_space=pltpu.VMEM),) * 2,
        scratch_shapes=[
            vmem((n_protos, block, depth), bf16),
            vmem((n_protos, block, depth), bf16),
            vmem((protos, depth), bf16),
            vmem((rows, protos), f32),
            vmem((rows, protos), f32),
            vmem((depth, rows), bf16),
            vmem((rows, LANES), f32),
            vmem((rows, LANES), f32),
            vmem((rows, LANES), f32),
            vmem((PASSES, 2, n_rows, 1, protos // 2), f32),
            vmem((1, protos), f32),
            vmem((PASSES, n_protos, 1, rows), f32),
            vmem((n_protos, 1, rows), f32),
            vmem((protos, depth), bf16),
            vmem((block, depth), bf16),
            vmem((block, depth), bf16),
            vmem((rows, protos), bf16),
            vmem((n_protos, block, depth), bf16),
            vmem((depth_z, LINES - 1, block, depth), bf16),
            vmem((depth_z, block, depth), bf16),
            vmem((depth_z, block, depth), bf16),
            vmem((4, 2, depth, half), bf16),
            vmem((4, 2, depth, half), bf16),
            vmem((2, depth, half), bf16),
            vmem((2, 2, half, depth), bf16),
            vmem((2, depth, half), bf16),
            vmem((2, 2, half, depth), bf16),
            vmem((4, 2, depth, half), f32),
            dma((3,)), dma((n_rows,)), dma, dma((depth_z - 1,)), dma((LINES - 1,)),
            dma, dma((depth_z - 1,)), dma((LINES - 1,)),
            dma((PASSES, 2)), dma((PASSES, 2)), dma((PASSES,)), dma((PASSES,)),
            dma, dma,
            dma((4, 2)), dma((4, 2)),
            dma((3, 2)), dma((2,)), dma((2, 2)),
            dma, dma((depth_z,)), dma, dma,
        ],
        compiler_params=pltpu.CompilerParams(
            collective_id=0, has_side_effects=True, vmem_limit_bytes=46 * 1024 * 1024
        ),
        name="head_step",
    )(*(pltpu.with_memory_space_constraint(v, pltpu.HBM) for v in (teacher_features, student_features, prototypes)))
    feature_grad, proto_grad = pl.pallas_call(
        store,
        out_shape=(
            jax.ShapeDtypeStruct((block, depth), f32),
            jax.ShapeDtypeStruct((chunk, depth), f32),
        ),
        in_specs=[pl.BlockSpec(memory_space=pltpu.VMEM)] * 2,
        out_specs=(pl.BlockSpec(memory_space=pl.ANY),) * 2,
        scratch_shapes=[dma, dma],
        compiler_params=pltpu.CompilerParams(vmem_limit_bytes=4 * 1024 * 1024),
        name="store",
    )(feature_grad, proto_grad)
    return feature_grad, proto_grad[None]


def solution(mesh):
    return jax.shard_map(
        on_device,
        mesh=mesh,
        in_specs=(P(("rows", "protos"), None), P(("rows", "protos"), None), P("protos", None)),
        out_specs=(P(("rows", "protos"), None), P("rows", "protos", None)),
        check_vma=False,
    )
```

```python
import functools
import math

import jax
import jax.numpy as jnp
from jax import lax
from jax.experimental import pallas as pl
from jax.experimental.pallas import tpu as pltpu
from jax.sharding import PartitionSpec as P

K = 131072
PASSES = 3
EPS = 1e-06
LANES = 128
STEP = 256
WIDE = 2048
MIDDLE = 512
CHIPS = 4
LINES = 4
MESH = pl.DeviceIdType.MESH
f32 = jnp.float32
bf16 = jnp.bfloat16


def unitize(values):
    values = values.astype(f32)
    return (values * lax.rsqrt(jnp.sum(values * values, axis=1, keepdims=True) + EPS)).astype(bf16)


def kernel(
    n_rows, n_protos, factor_rows,
    t_hbm, s_hbm, w_ref, fg_ref, pg_ref,
    tg, sg, uw, km, pm, st, rb, qb, acc, cbuf, cvec, rbuf, qbuf,
    wv, t_ref, s_ref, dall, fsend, fline, fout, frecv, psend, precv, xsend, xnear, relay, xrecv, pown,
    in_sem, turn_sem, t_ss, tz_rs, ty_rs, s_ss, sz_rs, sy_rs, c_ss, c_rs, r_ss, r_rs, q_ss, q_rs,
    p_ss, p_rs, x_ss, l_rs, x_rs, f_ss, fy_rs, g_ss, f_rs,
):
    rows, protos = km.shape
    depth = uw.shape[1]
    block = t_ref.shape[0]
    chunk = protos // n_rows
    half = chunk // 2
    scale = 1.5 * math.sqrt(depth)
    power = scale * math.log2(math.e)
    factor = scale * K / factor_rows
    r = lax.axis_index("rows")
    p = lax.axis_index("protos")

    loads = [
        pltpu.make_async_copy(source, target, in_sem.at[k])
        for k, (source, target) in enumerate(((t_hbm, t_ref), (s_hbm, s_ref), (w_ref, wv)))
    ]
    barrier = pltpu.get_barrier_semaphore()

    depth_z = n_protos // LINES
    y, z = lax.div(p, depth_z), lax.rem(p, depth_z)
    x, core = lax.div(r, 2), lax.rem(r, 2)

    def spot(dy, dz):
        return lax.rem(y + dy, LINES) * depth_z + lax.rem(z + dz, depth_z)

    def far_first(j):
        return depth_z // 2 + lax.div(j + 1, 2) * (1 - 2 * lax.rem(j, 2))

    def remote(source, target, send_sem, recv_sem, to):
        pltpu.make_async_remote_copy(
            src_ref=source, dst_ref=target, send_sem=send_sem, recv_sem=recv_sem,
            device_id=to, device_id_type=MESH,
        ).start()

    def greet(to):
        pl.semaphore_signal(barrier, inc=1, device_id=to, device_id_type=MESH)

    def all_protos(visit):
        def one(j, _):
            for dy in (2, 1, 3, 0):
                visit(spot(dy, far_first(j)))
            return 0

        lax.fori_loop(0, depth_z - 1, one, 0)
        for dy in (2, 1, 3):
            visit(spot(dy, 0))

    def all_rows(visit):
        for ahead in (2, 1, 3):
            for other in range(2):
                visit(lax.rem(x + ahead, CHIPS) * 2 + lax.rem(core + other, 2))
        visit(x * 2 + 1 - core)

    for dz in range(1, depth_z):
        greet({"protos": spot(0, dz)})
    for dy in range(1, LINES):
        greet({"protos": lax.rem(y + dy, LINES) * depth_z + z})
    all_rows(lambda q: greet({"rows": q}))
    for copy in loads:
        copy.start()

    def drain(view, sem):
        pltpu.make_async_copy(view, view, sem).wait()

    for copy in loads[:2]:
        copy.wait()
    tg[p] = unitize(t_ref[...])
    sg[p] = unitize(s_ref[...])
    pl.semaphore_wait(barrier, depth_z + LINES + n_rows - 3)

    def along_z(buf, send_sem, recv_sem):
        for j in reversed(range(depth_z - 1)):
            dz = depth_z // 2 + (j + 1) // 2 * (1 - 2 * (j % 2))
            remote(
                buf.at[p], buf.at[p], send_sem, recv_sem.at[dz - 1], {"protos": spot(0, dz)}
            )

    def along_y(buf, q, send_sem, recv_sem, distances):
        for dy in distances:
            to = lax.rem(y + dy, LINES) * depth_z + z
            remote(buf.at[q], buf.at[q], send_sem, recv_sem.at[dy - 1], {"protos": to})

    def pass_on(buf, send_sem, z_sem, y_sem):
        for j in reversed(range(depth_z - 1)):
            dz = depth_z // 2 + (j + 1) // 2 * (1 - 2 * (j % 2))
            q = spot(0, depth_z - dz)
            drain(buf.at[q], z_sem.at[dz - 1])
            along_y(buf, q, send_sem, y_sem, (1, 3, 2))

    def column_here(buf, dy, y_sem):
        line = lax.rem(y + LINES - dy, LINES) * depth_z
        drain(buf.at[pl.ds(line, depth_z)], y_sem.at[dy - 1])

    along_z(tg, t_ss, tz_rs)
    along_y(tg, p, t_ss, ty_rs, (1, 3, 2))
    loads[2].wait()

    def unit_step(i, _):
        at = pl.ds(pl.multiple_of(i * STEP, STEP), STEP)
        uw[at, :] = unitize(wv[at, :])
        return 0

    lax.fori_loop(0, protos // STEP, unit_step, 0)

    others = pl.ds(0, n_protos - 1)
    pass_on(tg, t_ss, tz_rs, ty_rs)
    along_z(sg, s_ss, sz_rs)
    def logits(left, i, width):
        at = pl.ds(pl.multiple_of(i * width, width), width)
        values = lax.dot_general(
            left, uw[at, :], (((1,), (1,)), ((), ())), preferred_element_type=f32
        )
        return at, jnp.exp2(values * power)

    pair_rows = 2 * depth_z * block

    def kernel_half(pair, c, first):
        lines = pl.ds(pair * 2 * depth_z, 2 * depth_z)
        here = pl.ds(pl.multiple_of(pair * pair_rows, pair_rows), pair_rows)
        teacher = tg[lines].reshape(pair_rows, depth)
        steps = protos // 2 // WIDE

        def one(i, _):
            at, values = logits(teacher, c * steps + i, WIDE)
            km[here, at] = values
            part = jnp.sum(values, axis=0, keepdims=True)
            to = pl.ds(pl.multiple_of(i * WIDE, WIDE), WIDE)
            cbuf[0, c, r, :, to] = part if first else cbuf[0, c, r, :, to] + part
            return 0

        lax.fori_loop(0, steps, one, 0)

    odd = lax.rem(y, 2)
    near = 3 - 2 * odd
    line = lax.rem(y + LINES - near, LINES) * depth_z
    drain(tg.at[pl.ds(line, depth_z)], ty_rs.at[near - 1])
    kernel_half(lax.div(y, 2), 0, True)
    kernel_half(lax.div(y, 2), 1, True)
    line = lax.rem(y + near, LINES) * depth_z
    drain(tg.at[pl.ds(line, depth_z)], ty_rs.at[LINES - near - 1])
    column_here(tg, 2, ty_rs)

    def column(values):
        return jnp.transpose(jnp.broadcast_to(values, (LANES, LANES)))

    def to_columns(values, ref):
        for g in range(rows // LANES):
            ref[g * LANES:(g + 1) * LANES, :] = column(values[:, g * LANES:(g + 1) * LANES])

    def lane_sums(acc, store, groups):
        for g in groups:
            turned = jnp.transpose(acc[g * LANES:(g + 1) * LANES, :])
            at = slice((g - groups[0]) * LANES, (g - groups[0] + 1) * LANES)
            store(at, jnp.sum(turned, axis=0, keepdims=True))

    tiles = protos // LANES
    groups = rows // LANES
    side = protos // 2

    def lane(j):
        return slice(j * LANES, (j + 1) * LANES)

    def rows_of(i):
        return pl.ds(pl.multiple_of(i * 8, 8), 8)

    def column_sweep(which):
        def one(i, sums):
            at = rows_of(i)
            value = rb[at, :]
            return tuple(s + km[at, lane(j)] * value for s, j in zip(sums, which))

        return lax.fori_loop(
            0, rows // 8, one, tuple(jnp.zeros((8, LANES), f32) for _ in which), unroll=4
        )

    def row_sweep(c):
        which = range(c * tiles // 2, (c + 1) * tiles // 2)
        cols = [jnp.broadcast_to(cvec[:, lane(j)], (8, LANES)) for j in which]

        def one(i, _):
            at = rows_of(i)
            parts = [km[at, lane(j)] * col for j, col in zip(which[:4], cols[:4])]
            for k in range(4, len(which)):
                parts[k % 4] = parts[k % 4] + km[at, lane(which[k])] * cols[k]
            total = (parts[0] + parts[1]) + (parts[2] + parts[3])
            acc[at, :] = total if c == 0 else acc[at, :] + total
            return 0

        lax.fori_loop(0, rows // 8, one, 0, unroll=4)

    def scale_both():
        cols = [jnp.broadcast_to(cvec[:, lane(j)], (8, LANES)) for j in range(tiles)]

        def one(i, _):
            at = rows_of(i)
            value = qb[at, :]
            for j in range(tiles):
                pm[at, lane(j)] = pm[at, lane(j)] * value
                km[at, lane(j)] = km[at, lane(j)] * cols[j]
            return 0

        lax.fori_loop(0, rows // 8, one, 0, unroll=2)

    def send_columns(step, c):
        mine = cbuf.at[step, c, r]
        sems = c_ss.at[step, c], c_rs.at[step, c]
        all_rows(lambda q: remote(mine, mine, *sems, {"rows": q}))

    def send_sums(step):
        mine = rbuf.at[step, p]
        sems = r_ss.at[step], r_rs.at[step]
        all_protos(lambda q: remote(mine, mine, *sems, {"protos": q}))

    def take_columns(step, c):
        drain(cbuf.at[step, c, pl.ds(0, n_rows - 1)], c_rs.at[step, c])
        cvec[:, c * side:(c + 1) * side] = 1.0 / jnp.sum(cbuf[step, c], axis=0)

    def take_sums(step):
        drain(rbuf.at[step, others], r_rs.at[step])
        to_columns(1.0 / jnp.sum(rbuf[step], axis=0), rb)

    def column_pass(step):
        take_sums(step - 1)
        for c in range(2):
            which = range(c * tiles // 2, (c + 1) * tiles // 2)
            for j, value in zip(which, column_sweep(which)):
                value = jnp.sum(value, axis=0, keepdims=True)
                cbuf[step, c, r, :, lane(j - which[0])] = value
            send_columns(step, c)

    def row_pass(step):
        for c in range(2):
            take_columns(step, c)
            row_sweep(c)

        def store(at, value):
            rbuf[step, p, :, at] = value

        lane_sums(acc, store, range(groups))
        send_sums(step)

    steps = protos // MIDDLE

    def student(begin, end):
        units = sg[...].reshape(rows, depth)

        def one(i, _):
            at, values = logits(units, i, MIDDLE)
            pm[:, at] = values
            qb[...] += sum(values[:, j * LANES:(j + 1) * LANES] for j in range(MIDDLE // LANES))
            return 0

        lax.fori_loop(begin, end, one, 0)

    def student_begin():
        for dy in (1, 2, 3):
            column_here(sg, dy, sy_rs)
        qb[...] = jnp.zeros_like(qb)
        student(0, steps // 2)

    def student_end():
        student(steps // 2, steps)

        def store(at, value):
            qbuf[p, :, at] = value

        lane_sums(qb, store, range(groups))
        all_protos(lambda q: remote(qbuf.at[p], qbuf.at[p], q_ss, q_rs, {"protos": q}))

    for c in range(2):
        kernel_half(1 - lax.div(y, 2), c, False)
        send_columns(0, c)

    along_y(sg, p, s_ss, sy_rs, (1, 3, 2))
    pass_on(sg, s_ss, sz_rs, sy_rs)

    chips = [lax.rem(x + ahead, CHIPS) for ahead in (2, 1, 3, 0)]
    places = [(0, 1), (0, 0), (1, 1), (2, 1), (1, 0), (2, 0), (3, 1), (3, 0)]
    owners = [chips[k] * 2 + lax.rem(core + other, 2) for k, other in places]

    def chunk_of(place):
        return pl.ds(pl.multiple_of(owners[place] * chunk, chunk), chunk)

    turns = [
        pltpu.make_async_copy(
            uw.at[chunk_of(k)], wv.at[pl.ds(k * chunk, chunk)], turn_sem.at[k]
        )
        for k in range(n_rows)
    ]

    for step in range(PASSES):
        if step > 0:
            column_pass(step)
        row_pass(step)
        if step == 0:
            student_begin()
            st[...] = jnp.transpose(sg[...].reshape(rows, depth).astype(f32)).astype(bf16)
        elif step == 1:
            student_end()
        else:
            drain(qbuf.at[others], q_rs)
            to_columns(1.0 / jnp.sum(qbuf[...], axis=0), qb)
            scale_both()
            for copy in turns:
                copy.start()
    take_sums(PASSES - 1)

    def send(source, target, send_sem, recv_sem, to):
        remote(source, target, send_sem, recv_sem, {"rows": to})

    up = lax.rem(x + 1, CHIPS) * 2 + core
    down = lax.rem(x + CHIPS - 1, CHIPS) * 2 + core
    mate = x * 2 + 1 - core

    def delta(place):
        at = chunk_of(place)
        to = slice(place * chunk, (place + 1) * chunk)
        for i in range(rows // 16):
            here = slice(i * 16, (i + 1) * 16)
            row = jnp.concatenate([rb[here, :]] * (chunk // LANES), axis=1)
            value = pm[here, at] - km[here, at] * row
            dall[here, to] = value.astype(bf16)

    def term(place, following=None):
        part = jnp.dot(
            st[...], dall[:, place * chunk:(place + 1) * chunk], preferred_element_type=f32
        )
        if following is not None:
            delta(following)
        k, other = places[place]
        if other:
            psend[k, 0] = part[:, :half].astype(bf16)
            psend[k, 1] = part[:, half:].astype(bf16)
            for h in range(2):
                send(psend.at[k, h], precv.at[k, h], p_ss.at[k, h], p_rs.at[k, h], mate)
        else:
            pown[k, 0] = part[:, :half]
            pown[k, 1] = part[:, half:]

    def joined(k, h):
        return pown[k, h] + precv[k, h].astype(f32)

    def features():
        half_rows = rows // 2

        def one(i, _):
            here = pl.ds(pl.multiple_of(i * half_rows, half_rows), half_rows)
            part = jnp.dot(dall[here, :], wv[...], preferred_element_type=f32).astype(bf16)
            to = pl.ds(i * (n_protos // 2), n_protos // 2)
            fsend[to] = part.reshape(n_protos // 2, block, depth)
            return 0

        lax.fori_loop(0, 2, one, 0)

        def post(j, _):
            dz = far_first(j)
            for dy in (2, 1, 3):
                q = spot(dy, dz)
                to = lax.rem(y + dy, LINES) * depth_z + z
                remote(fsend.at[q], fline.at[j, dy - 1], f_ss, fy_rs.at[j], {"protos": to})
            return 0

        lax.fori_loop(0, depth_z, post, 0)

    def features_on():
        def one(j, _):
            q = spot(0, far_first(j))
            drain(fline.at[j], fy_rs.at[j])
            value = fsend[q].astype(f32) + fline[j, 0].astype(f32)
            value = value + (fline[j, 1].astype(f32) + fline[j, 2].astype(f32))
            fout[j] = value.astype(bf16)
            return 0

        def step(j, _):
            one(j, 0)
            q = spot(0, far_first(j))
            remote(fout.at[j], frecv.at[z], g_ss, f_rs, {"protos": q})
            return 0

        lax.fori_loop(0, depth_z - 1, step, 0)
        one(depth_z - 1, 0)
        frecv[z] = fout[depth_z - 1]

    delta(0)
    for h in range(2):
        part = jnp.dot(
            st[...], dall[:, h * half:(h + 1) * half], preferred_element_type=f32
        )
        psend[0, h] = part.astype(bf16)
        send(psend.at[0, h], precv.at[0, h], p_ss.at[0, h], p_rs.at[0, h], mate)
        if h == 0:
            delta(1)
    term(1, 2)
    term(2, 3)
    for h, to in ((0, up), (1, down)):
        drain(precv.at[0, h], p_rs.at[0, h])
        xsend[h] = joined(0, h).astype(bf16)
        send(xsend.at[h], relay.at[h], x_ss.at[0, h], l_rs.at[h], to)
        if h == 0:
            term(3, 4)
    term(4, 5)
    term(5, 6)
    for k, h, to in ((1, 1, up), (2, 0, down)):
        drain(precv.at[k, h], p_rs.at[k, h])
        xnear[k - 1, h] = jnp.transpose(joined(k, h)).astype(bf16)
        send(xnear.at[k - 1, h], xrecv.at[k - 1, h], x_ss.at[k, h], x_rs.at[k - 1, h], to)
    term(6, 7)
    for copy in turns:
        copy.wait()
    features()
    term(7)
    for k, h, to in ((1, 0, up), (2, 1, down)):
        drain(precv.at[k, h], p_rs.at[k, h])
        drain(relay.at[h], l_rs.at[h])
        xnear[k - 1, h] = jnp.transpose(joined(k, h) + relay[h].astype(f32)).astype(bf16)
        send(xnear.at[k - 1, h], xrecv.at[k - 1, h], x_ss.at[k, h], x_rs.at[k - 1, h], to)

    features_on()
    for h in range(2):
        drain(precv.at[3, h], p_rs.at[3, h])
        pg_ref[h * half:(h + 1) * half, :] = jnp.transpose(joined(3, h))

    drain(tg.at[others], t_ss)
    drain(sg.at[others], s_ss)
    drain(qbuf.at[others], q_ss)
    for step in range(PASSES):
        for h in range(2):
            drain(cbuf.at[step, h, pl.ds(0, n_rows - 1)], c_ss.at[step, h])
        drain(rbuf.at[step, others], r_ss.at[step])
    for h in range(2):
        for k in range(4):
            drain(psend.at[k, h], p_ss.at[k, h])
        drain(xsend.at[h], x_ss.at[0, h])
    drain(fline, f_ss)

    drain(frecv.at[pl.ds(0, depth_z - 1)], f_rs)
    total = jnp.zeros((block, depth), f32)
    total = lax.fori_loop(0, depth_z, lambda i, a: a + frecv[i].astype(f32), total)
    fg_ref[...] = scale * total
    drain(frecv.at[pl.ds(0, depth_z - 1)], g_ss)

    for h in range(2):
        for line in range(2):
            drain(xrecv.at[line, h], x_rs.at[line, h])
    here = slice(0, chunk)
    received = [xrecv[line].reshape(chunk, depth).astype(f32) for line in range(2)]
    pg_ref[here, :] = factor * (pg_ref[here, :] + (received[0] + received[1]))
    for k in range(2):
        for h in range(2):
            drain(xnear.at[k, h], x_ss.at[k + 1, h])


def store(feature, proto, feature_out, proto_out, f_sem, p_sem):
    copies = [
        pltpu.make_async_copy(proto, proto_out, p_sem),
        pltpu.make_async_copy(feature, feature_out, f_sem),
    ]
    for copy in copies:
        copy.start()
    for copy in copies:
        copy.wait()


def on_device(teacher_features, student_features, prototypes):
    n_rows, n_protos = lax.axis_size("rows"), lax.axis_size("protos")
    block, depth = teacher_features.shape
    protos = prototypes.shape[0]
    rows = block * n_protos
    chunk = protos // n_rows
    half = chunk // 2
    depth_z = n_protos // LINES
    dma = pltpu.SemaphoreType.DMA
    vmem = pltpu.VMEM
    feature_grad, proto_grad = pl.pallas_call(
        functools.partial(kernel, n_rows, n_protos, rows * n_rows),
        out_shape=(
            jax.ShapeDtypeStruct((block, depth), f32),
            jax.ShapeDtypeStruct((chunk, depth), f32),
        ),
        in_specs=[pl.BlockSpec(memory_space=pltpu.HBM)] * 3,
        out_specs=(pl.BlockSpec(memory_space=pltpu.VMEM),) * 2,
        scratch_shapes=[
            vmem((n_protos, block, depth), bf16),
            vmem((n_protos, block, depth), bf16),
            vmem((protos, depth), bf16),
            vmem((rows, protos), f32),
            vmem((rows, protos), f32),
            vmem((depth, rows), bf16),
            vmem((rows, LANES), f32),
            vmem((rows, LANES), f32),
            vmem((rows, LANES), f32),
            vmem((PASSES, 2, n_rows, 1, protos // 2), f32),
            vmem((1, protos), f32),
            vmem((PASSES, n_protos, 1, rows), f32),
            vmem((n_protos, 1, rows), f32),
            vmem((protos, depth), bf16),
            vmem((block, depth), bf16),
            vmem((block, depth), bf16),
            vmem((rows, protos), bf16),
            vmem((n_protos, block, depth), bf16),
            vmem((depth_z, LINES - 1, block, depth), bf16),
            vmem((depth_z, block, depth), bf16),
            vmem((depth_z, block, depth), bf16),
            vmem((4, 2, depth, half), bf16),
            vmem((4, 2, depth, half), bf16),
            vmem((2, depth, half), bf16),
            vmem((2, 2, half, depth), bf16),
            vmem((2, depth, half), bf16),
            vmem((2, 2, half, depth), bf16),
            vmem((4, 2, depth, half), f32),
            dma((3,)), dma((n_rows,)), dma, dma((depth_z - 1,)), dma((LINES - 1,)),
            dma, dma((depth_z - 1,)), dma((LINES - 1,)),
            dma((PASSES, 2)), dma((PASSES, 2)), dma((PASSES,)), dma((PASSES,)),
            dma, dma,
            dma((4, 2)), dma((4, 2)),
            dma((3, 2)), dma((2,)), dma((2, 2)),
            dma, dma((depth_z,)), dma, dma,
        ],
        compiler_params=pltpu.CompilerParams(
            collective_id=0, has_side_effects=True, vmem_limit_bytes=46 * 1024 * 1024
        ),
        name="head_step",
    )(*(pltpu.with_memory_space_constraint(v, pltpu.HBM) for v in (teacher_features, student_features, prototypes)))
    feature_grad, proto_grad = pl.pallas_call(
        store,
        out_shape=(
            jax.ShapeDtypeStruct((block, depth), f32),
            jax.ShapeDtypeStruct((chunk, depth), f32),
        ),
        in_specs=[pl.BlockSpec(memory_space=pltpu.VMEM)] * 2,
        out_specs=(pl.BlockSpec(memory_space=pl.ANY),) * 2,
        scratch_shapes=[dma, dma],
        compiler_params=pltpu.CompilerParams(vmem_limit_bytes=4 * 1024 * 1024),
        name="store",
    )(feature_grad, proto_grad)
    return feature_grad, proto_grad[None]


def solution(mesh):
    return jax.shard_map(
        on_device,
        mesh=mesh,
        in_specs=(P(("rows", "protos"), None), P(("rows", "protos"), None), P("protos", None)),
        out_specs=(P(("rows", "protos"), None), P("rows", "protos", None)),
        check_vma=False,
    )
```

```python
import functools
import math

import jax
import jax.numpy as jnp
from jax import lax
from jax.experimental import pallas as pl
from jax.experimental.pallas import tpu as pltpu
from jax.sharding import PartitionSpec as P

K = 131072
PASSES = 3
EPS = 1e-06
LANES = 128
STEP = 256
WIDE = 2048
MIDDLE = 512
CHIPS = 4
LINES = 4
MESH = pl.DeviceIdType.MESH
f32 = jnp.float32
bf16 = jnp.bfloat16


def unitize(values):
    values = values.astype(f32)
    return (values * lax.rsqrt(jnp.sum(values * values, axis=1, keepdims=True) + EPS)).astype(bf16)


def kernel(
    n_rows, n_protos, factor_rows,
    t_hbm, s_hbm, w_ref, fg_ref, pg_ref,
    tg, sg, uw, km, pm, st, rb, qb, acc, cbuf, cvec, rbuf, qbuf,
    wv, t_ref, s_ref, dall, fsend, fline, fout, frecv, psend, precv, xsend, xnear, relay, xrecv, pown,
    in_sem, turn_sem, t_ss, tz_rs, ty_rs, s_ss, sz_rs, sy_rs, c_ss, c_rs, r_ss, r_rs, q_ss, q_rs,
    p_ss, p_rs, x_ss, l_rs, x_rs, f_ss, fy_rs, g_ss, f_rs,
):
    rows, protos = km.shape
    depth = uw.shape[1]
    block = t_ref.shape[0]
    chunk = protos // n_rows
    half = chunk // 2
    scale = 1.5 * math.sqrt(depth)
    power = scale * math.log2(math.e)
    factor = scale * K / factor_rows
    r = lax.axis_index("rows")
    p = lax.axis_index("protos")

    loads = [
        pltpu.make_async_copy(source, target, in_sem.at[k])
        for k, (source, target) in enumerate(((t_hbm, t_ref), (s_hbm, s_ref), (w_ref, wv)))
    ]
    barrier = pltpu.get_barrier_semaphore()

    depth_z = n_protos // LINES
    y, z = lax.div(p, depth_z), lax.rem(p, depth_z)
    x, core = lax.div(r, 2), lax.rem(r, 2)

    def spot(dy, dz):
        return lax.rem(y + dy, LINES) * depth_z + lax.rem(z + dz, depth_z)

    def far_first(j):
        return depth_z // 2 + lax.div(j + 1, 2) * (1 - 2 * lax.rem(j, 2))

    def remote(source, target, send_sem, recv_sem, to):
        pltpu.make_async_remote_copy(
            src_ref=source, dst_ref=target, send_sem=send_sem, recv_sem=recv_sem,
            device_id=to, device_id_type=MESH,
        ).start()

    def greet(to):
        pl.semaphore_signal(barrier, inc=1, device_id=to, device_id_type=MESH)

    def all_protos(visit):
        def one(j, _):
            for dy in (2, 1, 3, 0):
                visit(spot(dy, far_first(j)))
            return 0

        lax.fori_loop(0, depth_z - 1, one, 0)
        for dy in (2, 1, 3):
            visit(spot(dy, 0))

    def all_rows(visit):
        for ahead in (2, 1, 3):
            for other in range(2):
                visit(lax.rem(x + ahead, CHIPS) * 2 + lax.rem(core + other, 2))
        visit(x * 2 + 1 - core)

    for dz in range(1, depth_z):
        greet({"protos": spot(0, dz)})
    for dy in range(1, LINES):
        greet({"protos": lax.rem(y + dy, LINES) * depth_z + z})
    all_rows(lambda q: greet({"rows": q}))
    for copy in loads:
        copy.start()

    def drain(view, sem):
        pltpu.make_async_copy(view, view, sem).wait()

    for copy in loads[:2]:
        copy.wait()
    tg[p] = unitize(t_ref[...])
    sg[p] = unitize(s_ref[...])
    pl.semaphore_wait(barrier, depth_z + LINES + n_rows - 3)

    def along_z(buf, send_sem, recv_sem):
        for j in reversed(range(depth_z - 1)):
            dz = depth_z // 2 + (j + 1) // 2 * (1 - 2 * (j % 2))
            remote(
                buf.at[p], buf.at[p], send_sem, recv_sem.at[dz - 1], {"protos": spot(0, dz)}
            )

    def along_y(buf, q, send_sem, recv_sem, distances):
        for dy in distances:
            to = lax.rem(y + dy, LINES) * depth_z + z
            remote(buf.at[q], buf.at[q], send_sem, recv_sem.at[dy - 1], {"protos": to})

    def pass_on(buf, send_sem, z_sem, y_sem):
        for j in reversed(range(depth_z - 1)):
            dz = depth_z // 2 + (j + 1) // 2 * (1 - 2 * (j % 2))
            q = spot(0, depth_z - dz)
            drain(buf.at[q], z_sem.at[dz - 1])
            along_y(buf, q, send_sem, y_sem, (1, 3, 2))

    def column_here(buf, dy, y_sem):
        line = lax.rem(y + LINES - dy, LINES) * depth_z
        drain(buf.at[pl.ds(line, depth_z)], y_sem.at[dy - 1])

    along_z(tg, t_ss, tz_rs)
    along_y(tg, p, t_ss, ty_rs, (1, 3, 2))
    loads[2].wait()

    def unit_step(i, _):
        at = pl.ds(pl.multiple_of(i * STEP, STEP), STEP)
        uw[at, :] = unitize(wv[at, :])
        return 0

    lax.fori_loop(0, protos // STEP, unit_step, 0)

    others = pl.ds(0, n_protos - 1)
    pass_on(tg, t_ss, tz_rs, ty_rs)
    along_z(sg, s_ss, sz_rs)
    def logits(left, i, width):
        at = pl.ds(pl.multiple_of(i * width, width), width)
        values = lax.dot_general(
            left, uw[at, :], (((1,), (1,)), ((), ())), preferred_element_type=f32
        )
        return at, jnp.exp2(values * power)

    pair_rows = 2 * depth_z * block

    def kernel_half(pair, c, first):
        lines = pl.ds(pair * 2 * depth_z, 2 * depth_z)
        here = pl.ds(pl.multiple_of(pair * pair_rows, pair_rows), pair_rows)
        teacher = tg[lines].reshape(pair_rows, depth)
        steps = protos // 2 // WIDE

        def one(i, _):
            at, values = logits(teacher, c * steps + i, WIDE)
            km[here, at] = values
            part = jnp.sum(values, axis=0, keepdims=True)
            to = pl.ds(pl.multiple_of(i * WIDE, WIDE), WIDE)
            cbuf[0, c, r, :, to] = part if first else cbuf[0, c, r, :, to] + part
            return 0

        lax.fori_loop(0, steps, one, 0)

    odd = lax.rem(y, 2)
    near = 3 - 2 * odd
    line = lax.rem(y + LINES - near, LINES) * depth_z
    drain(tg.at[pl.ds(line, depth_z)], ty_rs.at[near - 1])
    kernel_half(lax.div(y, 2), 0, True)
    kernel_half(lax.div(y, 2), 1, True)
    line = lax.rem(y + near, LINES) * depth_z
    drain(tg.at[pl.ds(line, depth_z)], ty_rs.at[LINES - near - 1])
    column_here(tg, 2, ty_rs)

    def column(values):
        return jnp.transpose(jnp.broadcast_to(values, (LANES, LANES)))

    def to_columns(values, ref):
        for g in range(rows // LANES):
            ref[g * LANES:(g + 1) * LANES, :] = column(values[:, g * LANES:(g + 1) * LANES])

    def lane_sums(acc, store, groups):
        for g in groups:
            turned = jnp.transpose(acc[g * LANES:(g + 1) * LANES, :])
            at = slice((g - groups[0]) * LANES, (g - groups[0] + 1) * LANES)
            store(at, jnp.sum(turned, axis=0, keepdims=True))

    tiles = protos // LANES
    groups = rows // LANES
    side = protos // 2

    def lane(j):
        return slice(j * LANES, (j + 1) * LANES)

    def rows_of(i):
        return pl.ds(pl.multiple_of(i * 8, 8), 8)

    def column_sweep(which):
        sums = [jnp.zeros((8, LANES), f32) for _ in which]
        for i in range(rows // 8):
            at = slice(i * 8, (i + 1) * 8)
            value = rb[at, :]
            sums = [s + km[at, lane(j)] * value for s, j in zip(sums, which)]
        return sums

    def row_sweep(c):
        which = range(c * tiles // 2, (c + 1) * tiles // 2)
        cols = [jnp.broadcast_to(cvec[:, lane(j)], (8, LANES)) for j in which]

        def one(i):
            at = slice(i * 8, (i + 1) * 8)
            parts = [km[at, lane(j)] * col for j, col in zip(which[:4], cols[:4])]
            for k in range(4, len(which)):
                parts[k % 4] = parts[k % 4] + km[at, lane(which[k])] * cols[k]
            total = (parts[0] + parts[1]) + (parts[2] + parts[3])
            acc[at, :] = total if c == 0 else acc[at, :] + total

        for i in range(rows // 8):
            one(i)

    def scale_both():
        cols = [jnp.broadcast_to(cvec[:, lane(j)], (8, LANES)) for j in range(tiles)]

        def one(i, _):
            at = rows_of(i)
            value = qb[at, :]
            for j in range(tiles):
                pm[at, lane(j)] = pm[at, lane(j)] * value
                km[at, lane(j)] = km[at, lane(j)] * cols[j]
            return 0

        lax.fori_loop(0, rows // 8, one, 0, unroll=2)

    def send_columns(step, c):
        mine = cbuf.at[step, c, r]
        sems = c_ss.at[step, c], c_rs.at[step, c]
        all_rows(lambda q: remote(mine, mine, *sems, {"rows": q}))

    def send_sums(step):
        mine = rbuf.at[step, p]
        sems = r_ss.at[step], r_rs.at[step]
        all_protos(lambda q: remote(mine, mine, *sems, {"protos": q}))

    def take_columns(step, c):
        drain(cbuf.at[step, c, pl.ds(0, n_rows - 1)], c_rs.at[step, c])
        cvec[:, c * side:(c + 1) * side] = 1.0 / jnp.sum(cbuf[step, c], axis=0)

    def take_sums(step):
        drain(rbuf.at[step, others], r_rs.at[step])
        to_columns(1.0 / jnp.sum(rbuf[step], axis=0), rb)

    def column_pass(step):
        take_sums(step - 1)
        for c in range(2):
            which = range(c * tiles // 2, (c + 1) * tiles // 2)
            for j, value in zip(which, column_sweep(which)):
                value = jnp.sum(value, axis=0, keepdims=True)
                cbuf[step, c, r, :, lane(j - which[0])] = value
            send_columns(step, c)

    def row_pass(step):
        for c in range(2):
            take_columns(step, c)
            row_sweep(c)

        def store(at, value):
            rbuf[step, p, :, at] = value

        lane_sums(acc, store, range(groups))
        send_sums(step)

    steps = protos // MIDDLE

    def student(begin, end):
        units = sg[...].reshape(rows, depth)

        def one(i, _):
            at, values = logits(units, i, MIDDLE)
            pm[:, at] = values
            qb[...] += sum(values[:, j * LANES:(j + 1) * LANES] for j in range(MIDDLE // LANES))
            return 0

        lax.fori_loop(begin, end, one, 0)

    def student_begin():
        for dy in (1, 2, 3):
            column_here(sg, dy, sy_rs)
        qb[...] = jnp.zeros_like(qb)
        student(0, steps // 2)

    def student_end():
        student(steps // 2, steps)

        def store(at, value):
            qbuf[p, :, at] = value

        lane_sums(qb, store, range(groups))
        all_protos(lambda q: remote(qbuf.at[p], qbuf.at[p], q_ss, q_rs, {"protos": q}))

    for c in range(2):
        kernel_half(1 - lax.div(y, 2), c, False)
        send_columns(0, c)

    along_y(sg, p, s_ss, sy_rs, (1, 3, 2))
    pass_on(sg, s_ss, sz_rs, sy_rs)

    chips = [lax.rem(x + ahead, CHIPS) for ahead in (2, 1, 3, 0)]
    places = [(0, 1), (0, 0), (1, 1), (2, 1), (1, 0), (2, 0), (3, 1), (3, 0)]
    owners = [chips[k] * 2 + lax.rem(core + other, 2) for k, other in places]

    def chunk_of(place):
        return pl.ds(pl.multiple_of(owners[place] * chunk, chunk), chunk)

    turns = [
        pltpu.make_async_copy(
            uw.at[chunk_of(k)], wv.at[pl.ds(k * chunk, chunk)], turn_sem.at[k]
        )
        for k in range(n_rows)
    ]

    for step in range(PASSES):
        if step > 0:
            column_pass(step)
        row_pass(step)
        if step == 0:
            student_begin()
            st[...] = jnp.transpose(sg[...].reshape(rows, depth).astype(f32)).astype(bf16)
        elif step == 1:
            student_end()
        else:
            drain(qbuf.at[others], q_rs)
            to_columns(1.0 / jnp.sum(qbuf[...], axis=0), qb)
            scale_both()
            for copy in turns:
                copy.start()
    take_sums(PASSES - 1)

    def send(source, target, send_sem, recv_sem, to):
        remote(source, target, send_sem, recv_sem, {"rows": to})

    up = lax.rem(x + 1, CHIPS) * 2 + core
    down = lax.rem(x + CHIPS - 1, CHIPS) * 2 + core
    mate = x * 2 + 1 - core

    def delta(place, parts=range(rows // 16), columns=slice(0, chunk)):
        width = columns.stop - columns.start
        at = pl.ds(pl.multiple_of(owners[place] * chunk + columns.start, width), width)
        to = slice(place * chunk + columns.start, place * chunk + columns.stop)
        for i in parts:
            here = slice(i * 16, (i + 1) * 16)
            row = jnp.concatenate([rb[here, :]] * (width // LANES), axis=1)
            value = pm[here, at] - km[here, at] * row
            dall[here, to] = value.astype(bf16)

    def term(place, following=None):
        part = jnp.dot(
            st[...], dall[:, place * chunk:(place + 1) * chunk], preferred_element_type=f32
        )
        if following is not None:
            delta(following)
        k, other = places[place]
        if other:
            psend[k, 0] = part[:, :half].astype(bf16)
            psend[k, 1] = part[:, half:].astype(bf16)
            for h in range(2):
                send(psend.at[k, h], precv.at[k, h], p_ss.at[k, h], p_rs.at[k, h], mate)
        else:
            pown[k, 0] = part[:, :half]
            pown[k, 1] = part[:, half:]

    def joined(k, h):
        return pown[k, h] + precv[k, h].astype(f32)

    def features():
        half_rows = rows // 2

        def one(i, _):
            here = pl.ds(pl.multiple_of(i * half_rows, half_rows), half_rows)
            part = jnp.dot(dall[here, :], wv[...], preferred_element_type=f32).astype(bf16)
            to = pl.ds(i * (n_protos // 2), n_protos // 2)
            fsend[to] = part.reshape(n_protos // 2, block, depth)
            return 0

        lax.fori_loop(0, 2, one, 0)

        def post(j, _):
            dz = far_first(j)
            for dy in (2, 1, 3):
                q = spot(dy, dz)
                to = lax.rem(y + dy, LINES) * depth_z + z
                remote(fsend.at[q], fline.at[j, dy - 1], f_ss, fy_rs.at[j], {"protos": to})
            return 0

        lax.fori_loop(0, depth_z, post, 0)

    def features_on():
        def one(j, _):
            q = spot(0, far_first(j))
            drain(fline.at[j], fy_rs.at[j])
            value = fsend[q].astype(f32) + fline[j, 0].astype(f32)
            value = value + (fline[j, 1].astype(f32) + fline[j, 2].astype(f32))
            fout[j] = value.astype(bf16)
            return 0

        def step(j, _):
            one(j, 0)
            q = spot(0, far_first(j))
            remote(fout.at[j], frecv.at[z], g_ss, f_rs, {"protos": q})
            return 0

        lax.fori_loop(0, depth_z - 1, step, 0)
        one(depth_z - 1, 0)
        frecv[z] = fout[depth_z - 1]

    def first_half(h):
        part = jnp.dot(
            st[...], dall[:, h * half:(h + 1) * half], preferred_element_type=f32
        )
        psend[0, h] = part.astype(bf16)
        send(psend.at[0, h], precv.at[0, h], p_ss.at[0, h], p_rs.at[0, h], mate)

    delta(0, range(rows // 16), slice(0, half))
    first_half(0)

    @pl.when(p >= 0)
    def _():
        delta(0, range(rows // 16), slice(half, chunk))
        first_half(1)
        delta(1)

    term(1, 2)
    term(2, 3)
    for h, to in ((0, up), (1, down)):
        drain(precv.at[0, h], p_rs.at[0, h])
        xsend[h] = joined(0, h).astype(bf16)
        send(xsend.at[h], relay.at[h], x_ss.at[0, h], l_rs.at[h], to)
    term(3, 4)
    term(4, 5)
    term(5, 6)
    for k, h, to in ((1, 1, up), (2, 0, down)):
        drain(precv.at[k, h], p_rs.at[k, h])
        xnear[k - 1, h] = jnp.transpose(joined(k, h)).astype(bf16)
        send(xnear.at[k - 1, h], xrecv.at[k - 1, h], x_ss.at[k, h], x_rs.at[k - 1, h], to)
    term(6, 7)
    for copy in turns:
        copy.wait()
    features()
    term(7)
    for k, h, to in ((1, 0, up), (2, 1, down)):
        drain(precv.at[k, h], p_rs.at[k, h])
        drain(relay.at[h], l_rs.at[h])
        xnear[k - 1, h] = jnp.transpose(joined(k, h) + relay[h].astype(f32)).astype(bf16)
        send(xnear.at[k - 1, h], xrecv.at[k - 1, h], x_ss.at[k, h], x_rs.at[k - 1, h], to)

    features_on()
    for h in range(2):
        drain(precv.at[3, h], p_rs.at[3, h])
        pg_ref[h * half:(h + 1) * half, :] = jnp.transpose(joined(3, h))

    drain(tg.at[others], t_ss)
    drain(sg.at[others], s_ss)
    drain(qbuf.at[others], q_ss)
    for step in range(PASSES):
        for h in range(2):
            drain(cbuf.at[step, h, pl.ds(0, n_rows - 1)], c_ss.at[step, h])
        drain(rbuf.at[step, others], r_ss.at[step])
    for h in range(2):
        for k in range(4):
            drain(psend.at[k, h], p_ss.at[k, h])
        drain(xsend.at[h], x_ss.at[0, h])
    drain(fline, f_ss)

    drain(frecv.at[pl.ds(0, depth_z - 1)], f_rs)
    total = jnp.zeros((block, depth), f32)
    total = lax.fori_loop(0, depth_z, lambda i, a: a + frecv[i].astype(f32), total)
    fg_ref[...] = scale * total
    drain(frecv.at[pl.ds(0, depth_z - 1)], g_ss)

    for h in range(2):
        for line in range(2):
            drain(xrecv.at[line, h], x_rs.at[line, h])
    here = slice(0, chunk)
    received = [xrecv[line].reshape(chunk, depth).astype(f32) for line in range(2)]
    pg_ref[here, :] = factor * (pg_ref[here, :] + (received[0] + received[1]))
    for k in range(2):
        for h in range(2):
            drain(xnear.at[k, h], x_ss.at[k + 1, h])


def store(feature, proto, feature_out, proto_out, f_sem, p_sem):
    copies = [
        pltpu.make_async_copy(proto, proto_out, p_sem),
        pltpu.make_async_copy(feature, feature_out, f_sem),
    ]
    for copy in copies:
        copy.start()
    for copy in copies:
        copy.wait()


def on_device(teacher_features, student_features, prototypes):
    n_rows, n_protos = lax.axis_size("rows"), lax.axis_size("protos")
    block, depth = teacher_features.shape
    protos = prototypes.shape[0]
    rows = block * n_protos
    chunk = protos // n_rows
    half = chunk // 2
    depth_z = n_protos // LINES
    dma = pltpu.SemaphoreType.DMA
    vmem = pltpu.VMEM
    feature_grad, proto_grad = pl.pallas_call(
        functools.partial(kernel, n_rows, n_protos, rows * n_rows),
        out_shape=(
            jax.ShapeDtypeStruct((block, depth), f32),
            jax.ShapeDtypeStruct((chunk, depth), f32),
        ),
        in_specs=[pl.BlockSpec(memory_space=pltpu.HBM)] * 3,
        out_specs=(pl.BlockSpec(memory_space=pltpu.VMEM),) * 2,
        scratch_shapes=[
            vmem((n_protos, block, depth), bf16),
            vmem((n_protos, block, depth), bf16),
            vmem((protos, depth), bf16),
            vmem((rows, protos), f32),
            vmem((rows, protos), f32),
            vmem((depth, rows), bf16),
            vmem((rows, LANES), f32),
            vmem((rows, LANES), f32),
            vmem((rows, LANES), f32),
            vmem((PASSES, 2, n_rows, 1, protos // 2), f32),
            vmem((1, protos), f32),
            vmem((PASSES, n_protos, 1, rows), f32),
            vmem((n_protos, 1, rows), f32),
            vmem((protos, depth), bf16),
            vmem((block, depth), bf16),
            vmem((block, depth), bf16),
            vmem((rows, protos), bf16),
            vmem((n_protos, block, depth), bf16),
            vmem((depth_z, LINES - 1, block, depth), bf16),
            vmem((depth_z, block, depth), bf16),
            vmem((depth_z, block, depth), bf16),
            vmem((4, 2, depth, half), bf16),
            vmem((4, 2, depth, half), bf16),
            vmem((2, depth, half), bf16),
            vmem((2, 2, half, depth), bf16),
            vmem((2, depth, half), bf16),
            vmem((2, 2, half, depth), bf16),
            vmem((4, 2, depth, half), f32),
            dma((3,)), dma((n_rows,)), dma, dma((depth_z - 1,)), dma((LINES - 1,)),
            dma, dma((depth_z - 1,)), dma((LINES - 1,)),
            dma((PASSES, 2)), dma((PASSES, 2)), dma((PASSES,)), dma((PASSES,)),
            dma, dma,
            dma((4, 2)), dma((4, 2)),
            dma((3, 2)), dma((2,)), dma((2, 2)),
            dma, dma((depth_z,)), dma, dma,
        ],
        compiler_params=pltpu.CompilerParams(
            collective_id=0, has_side_effects=True, vmem_limit_bytes=46 * 1024 * 1024
        ),
        name="head_step",
    )(*(pltpu.with_memory_space_constraint(v, pltpu.HBM) for v in (teacher_features, student_features, prototypes)))
    feature_grad, proto_grad = pl.pallas_call(
        store,
        out_shape=(
            jax.ShapeDtypeStruct((block, depth), f32),
            jax.ShapeDtypeStruct((chunk, depth), f32),
        ),
        in_specs=[pl.BlockSpec(memory_space=pltpu.VMEM)] * 2,
        out_specs=(pl.BlockSpec(memory_space=pl.ANY),) * 2,
        scratch_shapes=[dma, dma],
        compiler_params=pltpu.CompilerParams(vmem_limit_bytes=4 * 1024 * 1024),
        name="store",
    )(feature_grad, proto_grad)
    return feature_grad, proto_grad[None]


def solution(mesh):
    return jax.shard_map(
        on_device,
        mesh=mesh,
        in_specs=(P(("rows", "protos"), None), P(("rows", "protos"), None), P("protos", None)),
        out_specs=(P(("rows", "protos"), None), P("rows", "protos", None)),
        check_vma=False,
    )
```
